512 devices in a mesh: ctx: 64 (over z_hi, y, x, core), tp: 8 (over z_lo).
Axes of the slice: x: 4, y: 4, z: 16 (z_hi: 2, z_lo: 8; z = z_hi * 8 + z_lo), core: 2. Of those that a mesh axis runs over, the one named last changes fastest.
Arguments:
- tokens: bfloat16 [16384, 4096], P('ctx', 'tp'), may hold values from -6 to 6
- norm_gain: bfloat16 [4096], P('tp'), may hold values from 0.25 to 1.75
- doc_ids: int32 [16384], P('ctx'), may hold values from 0 to 15, never falling along the last dimension, each value on 1 to 3840 neighbouring positions
- q_weight: bfloat16 [4096, 4096], P('ctx', 'tp'), may hold values from -0.09375 to 0.09375
- k_weight: bfloat16 [4096, 1024], P('ctx', 'tp'), may hold values from -0.09375 to 0.09375
- v_weight: bfloat16 [4096, 1024], P('ctx', 'tp'), may hold values from -0.09375 to 0.09375
- o_weight: bfloat16 [4096, 4096], P('tp', 'ctx'), may hold values from -0.09375 to 0.09375
Outputs:
- mixed: bfloat16 [16384, 4096], P('ctx', 'tp')
The draws below stay inside these ranges and needn't reach their ends.
Inputs may be any that keep to these rules, and one draw needn't show every extreme that they name: `doc_ids`: non-decreasing along the sequence; each document is a run of at most 3840 tokens and one run has exactly 3840.
All inputs are finite; a program needn't handle non-finite values.
Results may differ from the reference program's by a relative error of at most 0.015.
Values may be sent and summed in bfloat16 or wider, within the bound.
No kernel may reach another device: no remote copies, remote signals or barrier semaphores. Data moves between devices by JAX's collectives and lax.ppermute only.
A program may use at most 64 MiB of HBM per device.

```python
import math
import jax
import jax.numpy as jnp
import numpy as np
from jax import lax

D = 4096
HEADS = 32
KV_HEADS = 8
HEAD = 128
TOK_SHARD = 256
WIN = 16
TOKENS = 16384
DOC_MOST = 3840
DOCS = 16
N_CTX = 64
N_TP = 8


def draw_tokens(key, part):
    noise = jax.random.truncated_normal(jax.random.fold_in(key, 11), -6.0, 6.0, (TOKENS, D), jnp.float32)
    return noise.astype(jnp.bfloat16)


def draw_q_weight(key, part):
    noise = jax.random.truncated_normal(jax.random.fold_in(key, 17), -6.0, 6.0, (D, HEADS * HEAD), jnp.float32) / math.sqrt(D)
    return noise.astype(jnp.bfloat16)


def draw_k_weight(key, part):
    noise = jax.random.truncated_normal(jax.random.fold_in(key, 19), -6.0, 6.0, (D, KV_HEADS * HEAD), jnp.float32) / math.sqrt(D)
    return noise.astype(jnp.bfloat16)


def block_scale(stream_key, dims, pieces, low, largest):
    loudness = 1.0
    for dim, blocks in pieces:
        heights = jax.random.uniform(jax.random.fold_in(jax.random.fold_in(stream_key, 6), dim), (blocks,), jnp.float32, low / len(pieces), largest / len(pieces))
        loudness = loudness * jnp.repeat(jnp.exp(heights), dims[dim] // blocks).reshape((-1,) + (1,) * (len(dims) - 1 - dim))
    return loudness


def split_up(amount, total, most, skew):
    weights = [(1 << 20) // math.isqrt(grade ** skew) + 1 for grade in range(2, amount + 1)]
    surplus, holding = total - most - (amount - 1), [1] * (amount - 1)
    while surplus > 0:
        candidates = [i for i in range(amount - 1) if holding[i] < most]
        whole, budget = sum([weights[i] for i in candidates]), surplus
        for i in candidates:
            addition = min(most - holding[i], max(1, budget * weights[i] // whole), surplus)
            holding[i] = holding[i] + addition
            surplus = surplus - addition
    return np.array([most] + holding)


def uneven_parts(stream_key, number_of, total, most, slope):
    if number_of == 2:
        one = jax.random.randint(stream_key, (), max(1, total - most), min(most, total - 1) + 1)
        return jnp.stack([one, total - one])
    tallies = jnp.asarray(split_up(number_of, total, most, slope), jnp.int32)
    pairs = (number_of - 1) // 2
    giver, taker = tallies[1:1 + 2 * pairs:2], tallies[2:2 + 2 * pairs:2]
    room = jnp.minimum(giver - 1, most - taker)
    moved = jax.random.randint(jax.random.fold_in(stream_key, 1), (pairs,), 0, 1 << 20) % (room + 1)
    tallies = tallies.at[1:1 + 2 * pairs:2].set(giver - moved).at[2:2 + 2 * pairs:2].set(taker + moved)
    return tallies[jax.random.permutation(jax.random.fold_in(stream_key, 2), number_of)]


def normal_values(key, extent, width, most, cuts=(), kind=jnp.bfloat16):
    loudness = block_scale(key, extent, cuts, -0.22, 0.18) if cuts else 1.0
    values = jax.random.normal(key, extent, jnp.float32) * width * loudness
    return jnp.minimum(jnp.maximum(values, -most), most).astype(kind)


def setup_inputs(seed: int = 0) -> dict:
    arg_keys = jax.random.split(jax.random.key(seed), 8)
    tokens = draw_tokens(jax.random.fold_in(arg_keys[7], 71), 0)
    norm_gain = jnp.clip(1.0 + 0.15 * jax.random.normal(arg_keys[1], (D,), jnp.float32), 0.25, 1.75).astype(jnp.bfloat16)
    doc_ids = jnp.searchsorted(jnp.cumsum(uneven_parts(arg_keys[2], DOCS, TOKENS, DOC_MOST, 2)), jnp.arange(TOKENS), side="right").astype(jnp.int32)
    q_weight = draw_q_weight(jax.random.fold_in(arg_keys[7], 71), 0)
    k_weight = draw_k_weight(jax.random.fold_in(arg_keys[7], 71), 0)
    v_weight = normal_values(arg_keys[5], (D, KV_HEADS * HEAD), D ** -0.5, 0.09375, ((0, 64), (1, 8)))
    o_weight = normal_values(arg_keys[6], (HEADS * HEAD, D), (HEADS * HEAD) ** -0.5, 0.09375, ((0, 8), (1, 64)))
    return {"tokens": tokens, "norm_gain": norm_gain, "doc_ids": doc_ids, "q_weight": q_weight, "k_weight": k_weight, "v_weight": v_weight, "o_weight": o_weight}


def rotate(values, positions):
    half_dim = values.shape[-1] // 2
    inv_freq = 500000.0 ** (-(jnp.arange(half_dim, dtype=jnp.float32) * 2.0) / values.shape[-1])
    angles = positions[:, None] * inv_freq[None, :]
    cos_part = jnp.cos(angles)[:, None, :]
    sin_part = jnp.sin(angles)[:, None, :]
    first_half = values[..., :half_dim]
    second_half = values[..., half_dim:]
    return jnp.concatenate([first_half * cos_part - second_half * sin_part, second_half * cos_part + first_half * sin_part], axis=-1)

def reference(tokens, norm_gain, doc_ids, q_weight, k_weight, v_weight, o_weight):
    x_float = tokens.astype(jnp.float32)
    mean_sq = lax.optimization_barrier(jnp.mean(x_float * x_float, axis=-1, keepdims=True))
    normed = (x_float * lax.rsqrt(mean_sq + 1e-05) * norm_gain.astype(jnp.float32)).astype(jnp.bfloat16)
    query = jnp.dot(normed, q_weight, preferred_element_type=jnp.float32)
    key = jnp.dot(normed, k_weight, preferred_element_type=jnp.float32)
    value = jnp.dot(normed, v_weight, preferred_element_type=jnp.float32)
    positions = jnp.arange(TOKENS, dtype=jnp.int32).astype(jnp.float32)
    group_size = HEADS // KV_HEADS
    q_rot = rotate(query.reshape(TOKENS, HEADS, HEAD), positions).astype(jnp.bfloat16)
    k_rot = rotate(key.reshape(TOKENS, KV_HEADS, HEAD), positions).astype(jnp.bfloat16)
    v_low = value.astype(jnp.bfloat16).reshape(TOKENS, KV_HEADS, HEAD)
    lead = (WIN - 1) * TOK_SHARD
    k_pad = jnp.concatenate([jnp.zeros((lead, KV_HEADS, HEAD), jnp.bfloat16), k_rot], axis=0)
    v_pad = jnp.concatenate([jnp.zeros((lead, KV_HEADS, HEAD), jnp.bfloat16), v_low], axis=0)
    doc_pad = jnp.concatenate([jnp.full((lead,), -1, jnp.int32), doc_ids.astype(jnp.int32)], axis=0)
    scale = 1.0 / HEAD ** 0.5

    def one_shard(shard):
        first_row = (shard * TOK_SHARD).astype(jnp.int32)
        q_block = lax.dynamic_slice_in_dim(q_rot, first_row, TOK_SHARD, 0).astype(jnp.float32)
        q_block = q_block.reshape(TOK_SHARD, KV_HEADS, group_size, HEAD)
        q_docs = lax.dynamic_slice_in_dim(doc_ids.astype(jnp.int32), first_row, TOK_SHARD, 0)
        k_block = lax.dynamic_slice_in_dim(k_pad, first_row, WIN * TOK_SHARD, 0).astype(jnp.float32)
        v_block = lax.dynamic_slice_in_dim(v_pad, first_row, WIN * TOK_SHARD, 0).astype(jnp.float32)
        k_docs = lax.dynamic_slice_in_dim(doc_pad, first_row, WIN * TOK_SHARD, 0)
        q_pos = first_row + jnp.arange(TOK_SHARD, dtype=jnp.int32)
        k_pos = first_row - lead + jnp.arange(WIN * TOK_SHARD, dtype=jnp.int32)
        allowed = (k_pos[None, :] >= 0) & (k_pos[None, :] <= q_pos[:, None]) & (k_docs[None, :] == q_docs[:, None])
        scores = jnp.einsum('tkgd,skd->kgts', q_block, k_block) * scale
        masked = jnp.where(allowed[None, None], scores, -1e+30)
        top = lax.optimization_barrier(jnp.max(masked, axis=-1, keepdims=True))
        weights_exp = jnp.where(allowed[None, None], jnp.exp(scores - top), 0.0)
        total = lax.optimization_barrier(jnp.sum(weights_exp, axis=-1))
        weights_low = weights_exp.astype(jnp.bfloat16).astype(jnp.float32)
        summed = jnp.einsum('kgts,skd->tkgd', weights_low, v_block)
        result = summed / jnp.transpose(total, (2, 0, 1))[..., None]
        return result.reshape(TOK_SHARD, HEADS * HEAD).astype(jnp.bfloat16)
    attended = lax.map(one_shard, jnp.arange(N_CTX, dtype=jnp.int32)).reshape(TOKENS, HEADS * HEAD)
    group_cols = HEADS * HEAD // N_TP
    mixed = jnp.zeros((TOKENS, D), jnp.float32)
    for group in range(N_TP):
        partial_c = jnp.dot(attended[:, group * group_cols:(group + 1) * group_cols], o_weight[group * group_cols:(group + 1) * group_cols, :], preferred_element_type=jnp.float32)
        partial_c = lax.optimization_barrier(partial_c.astype(jnp.bfloat16))
        mixed = mixed + partial_c.astype(jnp.float32)
    return mixed.astype(jnp.bfloat16)
```

```python
import jax
import jax.numpy as jnp
from jax import lax
from jax.experimental import pallas as pl
from jax.experimental.pallas import tpu as pltpu
from jax.sharding import Mesh, PartitionSpec as P

HEAD = 128


def line(size, step):
    return [(i, i + step) for i in range(size) if 0 <= i + step < size]


def ring(size, step):
    return [(i, (i + step) % size) for i in range(size)]


def rotate(values, cos_part, sin_part):
    half_dim = values.shape[-1] // 2
    first_half = values[..., :half_dim]
    second_half = values[..., half_dim:]
    return jnp.concatenate(
        [
            first_half * cos_part - second_half * sin_part,
            second_half * cos_part + first_half * sin_part,
        ],
        axis=-1,
    )


def attention_kernel(q_ref, docs_ref, mine_ref, other_ref, out_ref, scores):
    group, rows, head = q_ref.shape
    q = q_ref[...].reshape(group * rows, head)
    factor = 1.4426950408889634 / head**0.5
    q_docs = docs_ref[...]
    tiles = [(mine_ref, s) for s in range(8)] + [(other_ref, s) for s in range(8)]
    top = None
    for n, (ref, s) in enumerate(tiles):
        keys = ref[s, :rows, :head]
        part = lax.dot_general(q, keys, (((1,), (1,)), ((), ())), preferred_element_type=jnp.float32)
        k_docs = ref[s, pl.ds(rows, 1), :].astype(jnp.float32)
        allowed = k_docs == q_docs
        if n == 7:
            q_at = lax.broadcasted_iota(jnp.int32, (rows, rows), 0)
            k_at = lax.broadcasted_iota(jnp.int32, (rows, rows), 1)
            allowed = allowed & (k_at <= q_at)
        part = jnp.where(allowed[None], part.reshape(group, rows, rows), -1e30)
        part = part.reshape(group * rows, rows)
        scores[:, n * rows : (n + 1) * rows] = part
        top = part if top is None else jnp.maximum(top, part)
    top = jnp.max(top, axis=1, keepdims=True)
    total = jnp.zeros((group * rows, rows), jnp.float32)
    summed = jnp.zeros((group * rows, head), jnp.float32)
    for n, (ref, s) in enumerate(tiles):
        expw = jnp.exp2((scores[:, n * rows : (n + 1) * rows] - top) * factor)
        total = total + expw
        summed = summed + jnp.dot(
            expw.astype(jnp.bfloat16), ref[s, :rows, head:], preferred_element_type=jnp.float32
        )
    result = (summed / jnp.sum(total, axis=1, keepdims=True)).astype(jnp.bfloat16)
    for g in range(group):
        out_ref[:, g * head : (g + 1) * head] = result[g * rows : (g + 1) * rows]


def local(tokens, norm_gain, doc_ids, q_weight, k_weight, v_weight, o_weight):
    rows, cols = tokens.shape
    n_tp = lax.axis_size("tp")
    q_cols = q_weight.shape[1]
    kv_cols = k_weight.shape[1]
    group = q_cols // HEAD
    tp = lax.axis_index("tp")
    zh, y, x, core = (lax.axis_index(a) for a in ("zh", "y", "x", "core"))
    shard = ((zh * 4 + y) * 4 + x) * 2 + core

    def both(block):
        away = lax.ppermute(block, "zh", [(0, 1), (1, 0)])
        return jnp.where(zh == 0, jnp.stack([block, away]), jnp.stack([away, block]))

    qkv_pair = both(jnp.concatenate([q_weight, k_weight, v_weight], axis=1))
    qkv = lax.all_gather(qkv_pair, ("y", "x", "core"), axis=1, tiled=True)
    qkv = qkv.reshape(-1, q_cols + 2 * kv_cols)
    o_pair = both(o_weight.T)
    o_rows = lax.all_gather(o_pair, ("y", "x", "core"), axis=1, tiled=True)
    o_rows = o_rows.reshape(-1, q_cols)

    block = jnp.concatenate([tokens, jnp.broadcast_to(norm_gain[None], (8, cols))], axis=0)
    whole = jnp.zeros((n_tp, rows + 8, cols), jnp.bfloat16)
    whole = lax.dynamic_update_slice(whole, block[None], (tp, 0, 0))
    for step in range(1, n_tp):
        away = lax.ppermute(block, "tp", ring(n_tp, step))
        whole = lax.dynamic_update_slice(whole, away[None], ((tp - step) % n_tp, 0, 0))
    x_float = whole[:, :rows].astype(jnp.float32)
    mean_sq = jnp.sum(x_float * x_float, axis=(0, 2), keepdims=True) / (n_tp * cols)
    gain = whole[:, rows : rows + 1].astype(jnp.float32)
    normed = (x_float * lax.rsqrt(mean_sq + 1e-05) * gain).astype(jnp.bfloat16)
    normed = jnp.transpose(normed, (1, 0, 2)).reshape(rows, n_tp * cols)
    projected = jnp.dot(normed, qkv, preferred_element_type=jnp.float32)

    inv_freq = 500000.0 ** (-(jnp.arange(HEAD // 2, dtype=jnp.float32) * 2.0) / HEAD)
    positions = (shard * rows + jnp.arange(rows, dtype=jnp.int32)).astype(jnp.float32)
    angles = positions[:, None] * inv_freq[None, :]
    cos_part, sin_part = jnp.cos(angles), jnp.sin(angles)
    key = rotate(projected[:, q_cols : q_cols + kv_cols], cos_part, sin_part)
    docs = doc_ids.astype(jnp.float32) + 1.0
    tile = jnp.concatenate(
        [
            jnp.concatenate([key, projected[:, q_cols + kv_cols :]], axis=1),
            jnp.broadcast_to(docs[None], (8, rows)),
        ],
        axis=0,
    ).astype(jnp.bfloat16)
    query = jnp.transpose(projected[:, :q_cols].reshape(rows, group, HEAD), (1, 0, 2))
    q_rot = rotate(query, cos_part[None], sin_part[None]).astype(jnp.bfloat16)

    back_1 = lax.ppermute(tile, ("zh", "y"), line(8, 1))
    back_2 = lax.ppermute(tile, ("zh", "y"), line(8, 2))
    mine = []
    for step in range(1, 4):
        pair = jnp.stack([back_1, jnp.where(x + step < 4, tile, back_2)])
        mine.append(lax.ppermute(pair, "x", ring(4, step)))
    mine.append(jnp.stack([back_1, tile]))
    sent = mine[:3] + [jnp.stack([back_1, jnp.where(core == 0, tile, back_2)])]
    other = lax.ppermute(jnp.concatenate(sent), "core", [(0, 1), (1, 0)])
    mine = jnp.concatenate(mine)

    attended = pl.pallas_call(
        attention_kernel,
        out_shape=jax.ShapeDtypeStruct((rows, q_cols), jnp.bfloat16),
        scratch_shapes=[pltpu.VMEM((group * rows, 16 * rows), jnp.float32)],
        name="attention",
    )(q_rot, docs[:, None], mine, other)

    partial_terms = lax.dot_general(
        attended,
        o_rows.reshape(n_tp, cols, q_cols),
        (((1,), (2,)), ((), ())),
        preferred_element_type=jnp.float32,
    )
    partial_terms = jnp.transpose(partial_terms, (1, 0, 2)).astype(jnp.bfloat16)
    return lax.psum_scatter(partial_terms, "tp", scatter_dimension=0, tiled=False)


def solution(mesh):
    fine = Mesh(mesh.devices.reshape(2, 4, 4, 2, 8), ("zh", "y", "x", "core", "tp"))
    ctx = ("zh", "y", "x", "core")
    return jax.shard_map(
        local,
        mesh=fine,
        in_specs=(
            P(ctx, "tp"),
            P("tp"),
            P(ctx),
            P(ctx, "tp"),
            P(ctx, "tp"),
            P(ctx, "tp"),
            P("tp", ctx),
        ),
        out_specs=P(ctx, "tp"),
        check_vma=False,
    )
```

```python
import jax
import jax.numpy as jnp
from jax import lax
from jax.experimental import pallas as pl
from jax.experimental.pallas import tpu as pltpu
from jax.sharding import Mesh, PartitionSpec as P

HEAD = 128
PLANE = ("y", "x", "core")


def line(size, step):
    return [(i, i + step) for i in range(size) if 0 <= i + step < size]


def ring(size, step):
    return [(i, (i + step) % size) for i in range(size)]


def plane_route(step, first):
    route = []
    for y in range(4):
        for x in range(4):
            for core in range(2):
                if (core == 0) == first:
                    to = (y * 4 + (x + step) % 4) * 2 + core
                else:
                    to = ((y + step) % 4 * 4 + x) * 2 + core
                route.append(((y * 4 + x) * 2 + core, to))
    return route


def block_rows(where, core, e, d, z):
    zh, y, x = where[0], where[1], where[2]
    far, near = (4 - e) % 4, (4 - d) % 4
    at_y = (y + jnp.where(core == 0, far, near)) % 4
    at_x = (x + jnp.where(core == 0, near, far)) % 4
    at_zh = jnp.where(zh == z, 0, 1)
    return pl.multiple_of((((at_zh * 4 + at_y) * 4 + at_x) * 2 + core) * 64, 64)


def load_weights(where, pieces, buffer, sem, first_col):
    cols = buffer.shape[1]
    copies = []
    for n, piece in enumerate(pieces):
        core = jnp.where(n < 4, where[3], 1 - where[3])
        for d in range(4):
            for z in range(2):
                rows = block_rows(where, core, n % 4, d, z)
                copies.append(
                    pltpu.make_async_copy(
                        piece.at[d, z, :, pl.ds(first_col, cols)], buffer.at[pl.ds(rows, 64)], sem.at[0]
                    )
                )
    for copy in copies:
        copy.start()
    return copies


def turn(values, cos_ref, sin_ref):
    return values * cos_ref[...] + pltpu.roll(values, HEAD // 2, 1) * sin_ref[...]


def kv_kernel(where, x_ref, docs_ref, cos_ref, sin_ref, *rest):
    pieces, (tile_ref, normed_ref, buffer, sem) = rest[:8], rest[8:]
    copies = load_weights(where, pieces, buffer, sem, 512)
    n_tp, rows, cols = normed_ref.shape
    square = jnp.zeros((rows, cols), jnp.float32)
    for j in range(n_tp):
        block = x_ref[j, :rows].astype(jnp.float32)
        square = square + block * block
    scale = lax.rsqrt(jnp.sum(square, axis=1, keepdims=True) / (n_tp * cols) + 1e-05)
    for j in range(n_tp):
        block = x_ref[j, :rows].astype(jnp.float32)
        gain = x_ref[j, pl.ds(rows, 1)].astype(jnp.float32)
        normed_ref[j] = (block * scale * gain).astype(jnp.bfloat16)
    for copy in copies:
        copy.wait()
    out = jnp.zeros((rows, 2 * HEAD), jnp.float32)
    for j in range(n_tp):
        out = out + jnp.dot(
            normed_ref[j], buffer[j * cols : (j + 1) * cols], preferred_element_type=jnp.float32
        )
    tile_ref[:rows, :HEAD] = turn(out[:, :HEAD], cos_ref, sin_ref).astype(jnp.bfloat16)
    tile_ref[:rows, HEAD:] = out[:, HEAD:].astype(jnp.bfloat16)
    tile_ref[rows:, :] = docs_ref[...]


def q_kernel(where, normed_ref, cos_ref, sin_ref, *rest):
    pieces, (q_ref, buffer, sem) = rest[:8], rest[8:]
    copies = load_weights(where, pieces, buffer, sem, 0)
    for copy in copies:
        copy.wait()
    n_tp, rows, cols = normed_ref.shape
    out = jnp.zeros((rows, buffer.shape[1]), jnp.float32)
    for j in range(n_tp):
        out = out + jnp.dot(
            normed_ref[j], buffer[j * cols : (j + 1) * cols], preferred_element_type=jnp.float32
        )
    for g in range(q_ref.shape[0]):
        head = out[:, g * HEAD : (g + 1) * HEAD]
        q_ref[g] = turn(head, cos_ref, sin_ref).astype(jnp.bfloat16)


def attention_kernel(q_ref, docs_ref, mine_ref, other_ref, out_ref, scores):
    group, rows, head = q_ref.shape
    q = q_ref[...].reshape(group * rows, head)
    factor = 1.4426950408889634 / head**0.5
    q_docs = docs_ref[...]
    tiles = [(mine_ref, s) for s in range(8)] + [(other_ref, s) for s in range(8)]
    top = None
    for n, (ref, s) in enumerate(tiles):
        keys = ref[s, :rows, :head]
        part = lax.dot_general(q, keys, (((1,), (1,)), ((), ())), preferred_element_type=jnp.float32)
        k_docs = ref[s, pl.ds(rows, 1), :].astype(jnp.float32)
        allowed = k_docs == q_docs
        if n == 7:
            q_at = lax.broadcasted_iota(jnp.int32, (rows, rows), 0)
            k_at = lax.broadcasted_iota(jnp.int32, (rows, rows), 1)
            allowed = allowed & (k_at <= q_at)
        part = jnp.where(allowed[None], part.reshape(group, rows, rows), -1e30)
        part = part.reshape(group * rows, rows)
        scores[:, n * rows : (n + 1) * rows] = part
        top = part if top is None else jnp.maximum(top, part)
    top = jnp.max(top, axis=1, keepdims=True)
    total = jnp.zeros((group * rows, rows), jnp.float32)
    summed = jnp.zeros((group * rows, head), jnp.float32)
    for n, (ref, s) in enumerate(tiles):
        expw = jnp.exp2((scores[:, n * rows : (n + 1) * rows] - top) * factor)
        total = total + expw
        summed = summed + jnp.dot(
            expw.astype(jnp.bfloat16), ref[s, :rows, head:], preferred_element_type=jnp.float32
        )
    result = (summed / jnp.sum(total, axis=1, keepdims=True)).astype(jnp.bfloat16)
    for g in range(group):
        out_ref[:, g * head : (g + 1) * head] = result[g * rows : (g + 1) * rows]


def out_kernel(pick, a_ref, o_ref, out_ref):
    del pick
    out_ref[0] = lax.dot_general(
        a_ref[...], o_ref[0], (((1,), (1,)), ((), ())), preferred_element_type=jnp.float32
    ).astype(jnp.bfloat16)


def local(tokens, norm_gain, doc_ids, q_weight, k_weight, v_weight, o_weight):
    rows, cols = tokens.shape
    n_tp = lax.axis_size("tp")
    q_cols = q_weight.shape[1]
    kv_cols = k_weight.shape[1]
    all_cols = q_cols + 2 * kv_cols
    group = q_cols // HEAD
    tp = lax.axis_index("tp")
    zh, y, x, core = (lax.axis_index(a) for a in ("zh", "y", "x", "core"))
    shard = ((zh * 4 + y) * 4 + x) * 2 + core
    where = jnp.stack([zh, y, x, core]).astype(jnp.int32)
    swap = [(0, 1), (1, 0)]

    block = jnp.concatenate([tokens, jnp.broadcast_to(norm_gain[None], (8, cols))], axis=0)
    whole = lax.all_gather(block, "tp", axis=0, tiled=False)

    weight = jnp.concatenate([q_weight, k_weight, v_weight], axis=1)
    pair = jnp.stack([weight, lax.ppermute(weight, "zh", swap)])
    near = [pair] + [lax.ppermute(pair, PLANE, plane_route(d, True)) for d in range(1, 4)]
    near = jnp.stack(near)
    o_block, near = lax.optimization_barrier((o_weight.T, near))
    pieces = [near] + [lax.ppermute(near, PLANE, plane_route(e, False)) for e in range(1, 4)]
    pieces = pieces + [lax.ppermute(piece, "core", swap) for piece in pieces]

    o_pair = jnp.stack([o_block, lax.ppermute(o_block, "zh", swap)])
    o_rows = lax.all_gather(o_pair, PLANE, axis=1, tiled=True)
    o_rows = o_rows.reshape(n_tp, cols, q_cols)

    inv_freq = 500000.0 ** (-(jnp.arange(HEAD // 2, dtype=jnp.float32) * 2.0) / HEAD)
    positions = (shard * rows + jnp.arange(rows, dtype=jnp.int32)).astype(jnp.float32)
    angles = positions[:, None] * inv_freq[None, :]
    cos_part, sin_part = jnp.cos(angles), jnp.sin(angles)
    cos_part = jnp.concatenate([cos_part, cos_part], axis=1)
    sin_part = jnp.concatenate([-sin_part, sin_part], axis=1)
    docs = doc_ids.astype(jnp.float32) + 1.0
    docs_rows = jnp.broadcast_to(docs[None].astype(jnp.bfloat16), (8, rows))

    vmem, hbm, smem = (pl.BlockSpec(memory_space=s) for s in (pltpu.VMEM, pl.ANY, pltpu.SMEM))
    tile, normed = pl.pallas_call(
        kv_kernel,
        out_shape=(
            jax.ShapeDtypeStruct((rows + 8, 2 * kv_cols), jnp.bfloat16),
            jax.ShapeDtypeStruct((n_tp, rows, cols), jnp.bfloat16),
        ),
        in_specs=[smem, vmem, vmem, vmem, vmem] + [hbm] * 8,
        scratch_shapes=[
            pltpu.VMEM((n_tp * cols, 2 * kv_cols), jnp.bfloat16),
            pltpu.SemaphoreType.DMA((1,)),
        ],
        name="kv_projection",
    )(where, whole, docs_rows, cos_part, sin_part, *pieces)
    q_rot = pl.pallas_call(
        q_kernel,
        out_shape=jax.ShapeDtypeStruct((group, rows, HEAD), jnp.bfloat16),
        in_specs=[smem, vmem, vmem, vmem] + [hbm] * 8,
        scratch_shapes=[
            pltpu.VMEM((n_tp * cols, q_cols), jnp.bfloat16),
            pltpu.SemaphoreType.DMA((1,)),
        ],
        cost_estimate=pl.CostEstimate(
            flops=2 * rows * n_tp * cols * q_cols, bytes_accessed=2 * n_tp * cols * (q_cols + rows), transcendentals=0
        ),
        name="q_projection",
    )(where, normed, cos_part, sin_part, *pieces)

    back_1 = lax.ppermute(tile, ("zh", "y"), line(8, 1))
    back_2 = lax.ppermute(tile, ("zh", "y"), line(8, 2))
    mine = []
    for step in range(1, 4):
        two = jnp.stack([back_1, jnp.where(x + step < 4, tile, back_2)])
        mine.append(lax.ppermute(two, "x", ring(4, step)))
    sent = mine + [jnp.stack([back_1, jnp.where(core == 0, tile, back_2)])]
    other = lax.ppermute(jnp.concatenate(sent), "core", swap)
    mine = jnp.concatenate(mine + [jnp.stack([back_1, tile])])

    attended = pl.pallas_call(
        attention_kernel,
        out_shape=jax.ShapeDtypeStruct((rows, q_cols), jnp.bfloat16),
        scratch_shapes=[pltpu.VMEM((group * rows, 16 * rows), jnp.float32)],
        name="attention",
    )(q_rot, docs[:, None], mine, other)

    parity, place = tp % 2, tp // 2

    def project(which):
        return pl.pallas_call(
            out_kernel,
            out_shape=jax.ShapeDtypeStruct((n_tp // 2, rows, cols), jnp.bfloat16),
            grid_spec=pltpu.PrefetchScalarGridSpec(
                num_scalar_prefetch=1,
                grid=(n_tp // 2,),
                in_specs=[
                    pl.BlockSpec((rows, q_cols), lambda m, pick: (0, 0)),
                    pl.BlockSpec(
                        (1, cols, q_cols),
                        lambda m, pick: ((2 * m + pick[0] + 4 * pick[1]) % 8, 0, 0),
                    ),
                ],
                out_specs=pl.BlockSpec((1, rows, cols), lambda m, pick: (m, 0, 0)),
            ),
            name="out_projection",
        )(jnp.stack([which, zh]).astype(jnp.int32), attended, o_rows)

    theirs = lax.ppermute(project(1 - parity), "tp", [(i, i ^ 1) for i in range(8)])
    ours = project(parity)
    ours = (ours.astype(jnp.float32) + theirs.astype(jnp.float32)).astype(jnp.bfloat16)
    mixed = lax.dynamic_index_in_dim(ours, place, 0, keepdims=False).astype(jnp.float32)
    for step in range(1, 4):
        piece = lax.dynamic_index_in_dim(ours, (place + step) % 4, 0, keepdims=False)
        route = [(i, 2 * ((i // 2 + step) % 4) + i % 2) for i in range(8)]
        mixed = mixed + lax.ppermute(piece, "tp", route).astype(jnp.float32)
    return mixed.astype(jnp.bfloat16)


def solution(mesh):
    fine = Mesh(mesh.devices.reshape(2, 4, 4, 2, 8), ("zh", "y", "x", "core", "tp"))
    ctx = ("zh", "y", "x", "core")
    return jax.shard_map(
        local,
        mesh=fine,
        in_specs=(
            P(ctx, "tp"),
            P("tp"),
            P(ctx),
            P(ctx, "tp"),
            P(ctx, "tp"),
            P(ctx, "tp"),
            P("tp", ctx),
        ),
        out_specs=P(ctx, "tp"),
        check_vma=False,
    )
```

```python
import jax
import jax.numpy as jnp
from jax import lax
from jax.experimental import pallas as pl
from jax.experimental.pallas import tpu as pltpu
from jax.sharding import Mesh, PartitionSpec as P

HEAD = 128
PLANE = ("y", "x", "core")


def line(size, step):
    return [(i, i + step) for i in range(size) if 0 <= i + step < size]


def ring(size, step):
    return [(i, (i + step) % size) for i in range(size)]


def plane_route(step, first):
    route = []
    for y in range(4):
        for x in range(4):
            for core in range(2):
                if (core == 0) == first:
                    to = (y * 4 + (x + step) % 4) * 2 + core
                else:
                    to = ((y + step) % 4 * 4 + x) * 2 + core
                route.append(((y * 4 + x) * 2 + core, to))
    return route


def block_rows(where, core, e, d, z):
    zh, y, x = where[0], where[1], where[2]
    far, near = (4 - e) % 4, (4 - d) % 4
    at_y = (y + jnp.where(core == 0, far, near)) % 4
    at_x = (x + jnp.where(core == 0, near, far)) % 4
    at_zh = jnp.where(zh == z, 0, 1)
    return pl.multiple_of((((at_zh * 4 + at_y) * 4 + at_x) * 2 + core) * 64, 64)


def load_weights(where, pieces, buffer, sem, first_col):
    cols = buffer.shape[1]
    copies = []
    for n, piece in enumerate(pieces):
        core = jnp.where(n < 4, where[3], 1 - where[3])
        for d in range(4):
            for z in range(2):
                rows = block_rows(where, core, n % 4, d, z)
                copies.append(
                    pltpu.make_async_copy(
                        piece.at[d, z, :, pl.ds(first_col, cols)], buffer.at[pl.ds(rows, 64)], sem.at[0]
                    )
                )
    for copy in copies:
        copy.start()
    return copies


def turn(values, cos_ref, sin_ref):
    return values * cos_ref[...] + pltpu.roll(values, HEAD // 2, 1) * sin_ref[...]


def kv_kernel(where, x_ref, docs_ref, cos_ref, sin_ref, *rest):
    pieces, (tile_ref, normed_ref, buffer, sem) = rest[:8], rest[8:]
    copies = load_weights(where, pieces, buffer, sem, 512)
    n_tp, _, cols = x_ref.shape
    rows = normed_ref.shape[0]
    square = jnp.zeros((rows, cols), jnp.float32)
    for j in range(n_tp):
        block = x_ref[j, :rows].astype(jnp.float32)
        square = square + block * block
    scale = lax.rsqrt(jnp.sum(square, axis=1, keepdims=True) / (n_tp * cols) + 1e-05)
    for j in range(n_tp):
        block = x_ref[j, :rows].astype(jnp.float32)
        gain = x_ref[j, pl.ds(rows, 1)].astype(jnp.float32)
        normed_ref[:, j * cols : (j + 1) * cols] = (block * scale * gain).astype(jnp.bfloat16)
    for copy in copies:
        copy.wait()
    out = jnp.dot(normed_ref[...], buffer[...], preferred_element_type=jnp.float32)
    tile_ref[:rows, :HEAD] = turn(out[:, :HEAD], cos_ref, sin_ref).astype(jnp.bfloat16)
    tile_ref[:rows, HEAD:] = out[:, HEAD:].astype(jnp.bfloat16)
    tile_ref[rows:, :] = docs_ref[...]


def q_kernel(where, normed_ref, cos_ref, sin_ref, *rest):
    pieces, (q_ref, buffer, sem) = rest[:8], rest[8:]
    copies = load_weights(where, pieces, buffer, sem, 0)
    for copy in copies:
        copy.wait()
    out = jnp.dot(normed_ref[...], buffer[...], preferred_element_type=jnp.float32)
    factor = 1.4426950408889634 / HEAD**0.5
    for g in range(q_ref.shape[0]):
        head = turn(out[:, g * HEAD : (g + 1) * HEAD], cos_ref, sin_ref)
        q_ref[g] = (head * factor).astype(jnp.bfloat16)


def attention_kernel(q_ref, docs_ref, mine_ref, other_ref, out_ref, scores):
    group, rows, head = q_ref.shape
    q_docs = docs_ref[...]
    ones = jnp.ones((8, rows, head), jnp.bfloat16)
    for g in range(group):
        at = slice(g * rows, (g + 1) * rows)
        top = None
        for n in range(16):
            ref, s = (mine_ref, n) if n < 8 else (other_ref, n - 8)
            part = lax.dot_general(
                q_ref[g],
                ref[s, :rows, :head],
                (((1,), (1,)), ((), ())),
                preferred_element_type=jnp.float32,
            )
            allowed = ref[s, pl.ds(rows, 1), :].astype(jnp.float32) == q_docs
            if n == 7:
                q_at = lax.broadcasted_iota(jnp.int32, (rows, rows), 0)
                k_at = lax.broadcasted_iota(jnp.int32, (rows, rows), 1)
                allowed = allowed & (k_at <= q_at)
            part = jnp.where(allowed, part, -1e30)
            scores[at, n * rows : (n + 1) * rows] = part
            most = jnp.maximum(part[:, :head], part[:, head:])
            top = most if top is None else jnp.maximum(top, most)
        top = jnp.max(top, axis=1, keepdims=True)
        expw = jnp.exp2(scores[at, :] - top).astype(jnp.bfloat16)
        summed = jnp.zeros((rows, 2 * head), jnp.float32)
        for n, ref in enumerate((mine_ref, other_ref)):
            values = jnp.concatenate([ref[:, :rows, head:], ones], axis=2)
            values = values.reshape(8 * rows, 2 * head)
            summed = summed + jnp.dot(
                expw[:, n * 8 * rows : (n + 1) * 8 * rows], values, preferred_element_type=jnp.float32
            )
        out_ref[:, g * head : (g + 1) * head] = (summed[:, :head] / summed[:, head:]).astype(
            jnp.bfloat16
        )


def out_kernel(zh, a_ref, o_ref, out_ref):
    del zh
    out_ref[0] = lax.dot_general(
        a_ref[...], o_ref[0], (((1,), (1,)), ((), ())), preferred_element_type=jnp.float32
    ).astype(jnp.bfloat16)


def local(tokens, norm_gain, doc_ids, q_weight, k_weight, v_weight, o_weight):
    rows, cols = tokens.shape
    n_tp = lax.axis_size("tp")
    q_cols = q_weight.shape[1]
    kv_cols = k_weight.shape[1]
    all_cols = q_cols + 2 * kv_cols
    group = q_cols // HEAD
    zh, y, x, core = (lax.axis_index(a) for a in ("zh", "y", "x", "core"))
    shard = ((zh * 4 + y) * 4 + x) * 2 + core
    where = jnp.stack([zh, y, x, core]).astype(jnp.int32)
    swap = [(0, 1), (1, 0)]

    block = jnp.concatenate([tokens, jnp.broadcast_to(norm_gain[None], (8, cols))], axis=0)
    whole = lax.all_gather(block, "tp", axis=0, tiled=False)

    weight = jnp.concatenate([q_weight, k_weight, v_weight], axis=1)
    pair = jnp.stack([weight, lax.ppermute(weight, "zh", swap)])
    near = [pair] + [lax.ppermute(pair, PLANE, plane_route(d, True)) for d in range(1, 4)]
    near = jnp.stack(near)
    pieces = [near] + [lax.ppermute(near, PLANE, plane_route(e, False)) for e in range(1, 4)]

    o_block = o_weight.T
    o_away, pieces[3] = lax.optimization_barrier((lax.ppermute(o_block, "zh", swap), pieces[3]))
    o_pair = jnp.stack([o_block, o_away])
    pieces = pieces + [lax.ppermute(piece, "core", swap) for piece in pieces]
    o_rows = lax.all_gather(o_pair, PLANE, axis=1, tiled=True)
    o_rows = o_rows.reshape(n_tp, cols, q_cols)

    inv_freq = 500000.0 ** (-(jnp.arange(HEAD // 2, dtype=jnp.float32) * 2.0) / HEAD)
    positions = (shard * rows + jnp.arange(rows, dtype=jnp.int32)).astype(jnp.float32)
    angles = positions[:, None] * inv_freq[None, :]
    cos_part, sin_part = jnp.cos(angles), jnp.sin(angles)
    cos_part = jnp.concatenate([cos_part, cos_part], axis=1)
    sin_part = jnp.concatenate([-sin_part, sin_part], axis=1)
    docs = doc_ids.astype(jnp.float32) + 1.0
    docs_rows = jnp.broadcast_to(docs[None].astype(jnp.bfloat16), (8, rows))

    vmem, hbm, smem = (pl.BlockSpec(memory_space=s) for s in (pltpu.VMEM, pl.ANY, pltpu.SMEM))
    tile, normed = pl.pallas_call(
        kv_kernel,
        out_shape=(
            jax.ShapeDtypeStruct((rows + 8, 2 * kv_cols), jnp.bfloat16),
            jax.ShapeDtypeStruct((rows, n_tp * cols), jnp.bfloat16),
        ),
        in_specs=[smem, vmem, vmem, vmem, vmem] + [hbm] * 8,
        scratch_shapes=[
            pltpu.VMEM((n_tp * cols, 2 * kv_cols), jnp.bfloat16),
            pltpu.SemaphoreType.DMA((1,)),
        ],
        name="kv_projection",
    )(where, whole, docs_rows, cos_part, sin_part, *pieces)
    q_rot = pl.pallas_call(
        q_kernel,
        out_shape=jax.ShapeDtypeStruct((group, rows, HEAD), jnp.bfloat16),
        in_specs=[smem, vmem, vmem, vmem] + [hbm] * 8,
        scratch_shapes=[
            pltpu.VMEM((n_tp * cols, q_cols), jnp.bfloat16),
            pltpu.SemaphoreType.DMA((1,)),
        ],
        cost_estimate=pl.CostEstimate(
            flops=2 * rows * n_tp * cols * q_cols, bytes_accessed=2 * n_tp * cols * (q_cols + rows), transcendentals=0
        ),
        name="q_projection",
    )(where, normed, cos_part, sin_part, *pieces)

    back_1 = lax.ppermute(tile, ("zh", "y"), line(8, 1))
    back_2 = lax.ppermute(tile, ("zh", "y"), line(8, 2))
    back_1, back_2, q_rot = lax.optimization_barrier((back_1, back_2, q_rot))
    mine = []
    for step in range(1, 4):
        two = jnp.stack([back_1, jnp.where(x + step < 4, tile, back_2)])
        mine.append(lax.ppermute(two, "x", ring(4, step)))
    sent = mine + [jnp.stack([back_1, jnp.where(core == 0, tile, back_2)])]
    other = lax.ppermute(jnp.concatenate(sent), "core", swap)
    mine = jnp.concatenate(mine + [jnp.stack([back_1, tile])])

    attended = pl.pallas_call(
        attention_kernel,
        out_shape=jax.ShapeDtypeStruct((rows, q_cols), jnp.bfloat16),
        in_specs=[vmem] * 4,
        scratch_shapes=[pltpu.VMEM((group * rows, 16 * rows), jnp.float32)],
        name="attention",
    )(q_rot, docs[:, None], mine, other)

    partial_terms = pl.pallas_call(
        out_kernel,
        out_shape=jax.ShapeDtypeStruct((n_tp, rows, cols), jnp.bfloat16),
        grid_spec=pltpu.PrefetchScalarGridSpec(
            num_scalar_prefetch=1,
            grid=(n_tp,),
            in_specs=[
                pl.BlockSpec((rows, q_cols), lambda m, zh: (0, 0)),
                pl.BlockSpec((1, cols, q_cols), lambda m, zh: ((m + 4 * zh[0]) % 8, 0, 0)),
            ],
            out_specs=pl.BlockSpec((1, rows, cols), lambda m, zh: (m, 0, 0)),
        ),
        name="out_projection",
    )(where[:1], attended, o_rows)
    return lax.psum_scatter(
        partial_terms.reshape(n_tp * rows, cols), "tp", scatter_dimension=0, tiled=True
    )


def solution(mesh):
    fine = Mesh(mesh.devices.reshape(2, 4, 4, 2, 8), ("zh", "y", "x", "core", "tp"))
    ctx = ("zh", "y", "x", "core")
    return jax.shard_map(
        local,
        mesh=fine,
        in_specs=(
            P(ctx, "tp"),
            P("tp"),
            P(ctx),
            P(ctx, "tp"),
            P(ctx, "tp"),
            P(ctx, "tp"),
            P("tp", ctx),
        ),
        out_specs=P(ctx, "tp"),
        check_vma=False,
    )
```

```python
import jax
import jax.numpy as jnp
from jax import lax
from jax.experimental import pallas as pl
from jax.experimental.pallas import tpu as pltpu
from jax.sharding import Mesh, PartitionSpec as P


HEAD = 128
PLANE = ("y", "x", "core")
FOLDED = [0, 2, 4, 6, 7, 5, 3, 1]


def line(size, step):
    return [(i, i + step) for i in range(size) if 0 <= i + step < size]


def ring(size, step):
    return [(i, (i + step) % size) for i in range(size)]


def two_back():
    route = []
    for row in range(6):
        for tp in range(8):
            to = (tp + 1) % 8 if row in (2, 3) else tp
            route.append((row * 8 + tp, (row + 2) * 8 + to))
    return route


def settle():
    return [(row * 8 + (tp + 1) % 8, row * 8 + tp) for row in (4, 5) for tp in range(8)]


def plane_route(step, first):
    route = []
    for y in range(4):
        for x in range(4):
            for core in range(2):
                if (core == 0) == first:
                    to = (y * 4 + (x + step) % 4) * 2 + core
                else:
                    to = ((y + step) % 4 * 4 + x) * 2 + core
                route.append(((y * 4 + x) * 2 + core, to))
    return route


def block_rows(where, core, e, d, z):
    zh, y, x = where[0], where[1], where[2]
    far, near = (4 - e) % 4, (4 - d) % 4
    at_y = (y + jnp.where(core == 0, far, near)) % 4
    at_x = (x + jnp.where(core == 0, near, far)) % 4
    at_zh = jnp.where(zh == z, 0, 1)
    return pl.multiple_of((((at_zh * 4 + at_y) * 4 + at_x) * 2 + core) * 64, 64)


def load_weights(where, pieces, buffer, sem, first_col):
    cols = buffer.shape[1]
    copies = []
    for n, piece in enumerate(pieces):
        core = jnp.where(n < 4, where[3], 1 - where[3])
        for d in range(4):
            for z in range(2):
                rows = block_rows(where, core, n % 4, d, z)
                copies.append(
                    pltpu.make_async_copy(
                        piece.at[d, z, :, pl.ds(first_col, cols)], buffer.at[pl.ds(rows, 64)], sem.at[0]
                    )
                )
    for copy in copies:
        copy.start()
    return copies


def turn(values, cos_ref, sin_ref):
    return values * cos_ref[...] + pltpu.roll(values, HEAD // 2, 1) * sin_ref[...]


def kv_kernel(where, x_ref, docs_ref, cos_ref, sin_ref, *rest):
    pieces, (tile_ref, normed_ref, buffer, sem) = rest[:8], rest[8:]
    copies = load_weights(where, pieces, buffer, sem, 512)
    n_tp, _, cols = x_ref.shape
    rows = normed_ref.shape[0]
    square = jnp.zeros((rows, cols), jnp.float32)
    for j in range(n_tp):
        block = x_ref[j, :rows].astype(jnp.float32)
        square = square + block * block
    scale = lax.rsqrt(jnp.sum(square, axis=1, keepdims=True) / (n_tp * cols) + 1e-05)
    for j in range(n_tp):
        block = x_ref[j, :rows].astype(jnp.float32)
        gain = x_ref[j, pl.ds(rows, 1)].astype(jnp.float32)
        at = FOLDED[j] * cols
        normed_ref[:, at : at + cols] = (block * scale * gain).astype(jnp.bfloat16)
    for copy in copies:
        copy.wait()
    out = jnp.dot(normed_ref[...], buffer[...], preferred_element_type=jnp.float32)
    tile_ref[:rows, :HEAD] = turn(out[:, :HEAD], cos_ref, sin_ref).astype(jnp.bfloat16)
    tile_ref[:rows, HEAD:] = out[:, HEAD:].astype(jnp.bfloat16)
    tile_ref[rows:, :] = docs_ref[...]


def q_kernel(where, normed_ref, cos_ref, sin_ref, *rest):
    pieces, (q_ref, buffer, sem) = rest[:8], rest[8:]
    copies = load_weights(where, pieces, buffer, sem, 0)
    for copy in copies:
        copy.wait()
    out = jnp.dot(normed_ref[...], buffer[...], preferred_element_type=jnp.float32)
    factor = 1.4426950408889634 / HEAD**0.5
    for g in range(q_ref.shape[0]):
        head = turn(out[:, g * HEAD : (g + 1) * HEAD], cos_ref, sin_ref)
        q_ref[g] = (head * factor).astype(jnp.bfloat16)


def attention_kernel(q_ref, docs_ref, mine_ref, other_ref, out_ref, scores):
    group, rows, head = q_ref.shape
    q_docs = docs_ref[...]
    ones = jnp.ones((8, rows, head), jnp.bfloat16)
    for g in range(group):
        at = slice(g * rows, (g + 1) * rows)
        top = None
        for n in range(16):
            ref, s = (mine_ref, n) if n < 8 else (other_ref, n - 8)
            part = lax.dot_general(
                q_ref[g],
                ref[s, :rows, :head],
                (((1,), (1,)), ((), ())),
                preferred_element_type=jnp.float32,
            )
            allowed = ref[s, pl.ds(rows, 1), :].astype(jnp.float32) == q_docs
            if n == 7:
                q_at = lax.broadcasted_iota(jnp.int32, (rows, rows), 0)
                k_at = lax.broadcasted_iota(jnp.int32, (rows, rows), 1)
                allowed = allowed & (k_at <= q_at)
            part = jnp.where(allowed, part, -1e30)
            scores[at, n * rows : (n + 1) * rows] = part
            most = jnp.maximum(part[:, :head], part[:, head:])
            top = most if top is None else jnp.maximum(top, most)
        top = jnp.max(top, axis=1, keepdims=True)
        expw = jnp.exp2(scores[at, :] - top).astype(jnp.bfloat16)
        summed = jnp.zeros((rows, 2 * head), jnp.float32)
        for n, ref in enumerate((mine_ref, other_ref)):
            values = jnp.concatenate([ref[:, :rows, head:], ones], axis=2)
            values = values.reshape(8 * rows, 2 * head)
            summed = summed + jnp.dot(
                expw[:, n * 8 * rows : (n + 1) * 8 * rows], values, preferred_element_type=jnp.float32
            )
        out_ref[:, g * head : (g + 1) * head] = (summed[:, :head] / summed[:, head:]).astype(
            jnp.bfloat16
        )


def out_kernel(order, a_ref, o_ref, out_ref):
    del order
    out_ref[0] = lax.dot_general(
        a_ref[...], o_ref[0], (((1,), (1,)), ((), ())), preferred_element_type=jnp.float32
    ).astype(jnp.bfloat16)


def local(tokens, norm_gain, doc_ids, q_weight, k_weight, v_weight, o_weight):
    rows, cols = tokens.shape
    n_tp = lax.axis_size("tp")
    q_cols = q_weight.shape[1]
    kv_cols = k_weight.shape[1]
    group = q_cols // HEAD
    zh, y, x, core = (lax.axis_index(a) for a in ("zh", "y", "x", "core"))
    shard = ((zh * 4 + y) * 4 + x) * 2 + core
    where = jnp.stack([zh, y, x, core]).astype(jnp.int32)
    swap = [(0, 1), (1, 0)]

    block = jnp.concatenate([tokens, jnp.broadcast_to(norm_gain[None], (8, cols))], axis=0)
    whole = lax.all_gather(block, "tp", axis=0, tiled=False, axis_index_groups=[FOLDED])

    weight = jnp.concatenate([q_weight, k_weight, v_weight], axis=1)
    away = lax.ppermute(weight, "zh", swap)
    pair = jnp.stack([weight, away])
    near = [pair] + [lax.ppermute(pair, PLANE, plane_route(d, True)) for d in range(1, 4)]
    near = jnp.stack(near)
    pieces = [near] + [lax.ppermute(near, PLANE, plane_route(e, False)) for e in range(1, 4)]

    o_block = o_weight.T
    o_away = lax.ppermute(o_block, "zh", swap)
    o_pair = jnp.stack([o_block, o_away])
    pieces = pieces + [lax.ppermute(piece, "core", swap) for piece in pieces]
    o_rows = lax.all_gather(o_pair, PLANE, axis=1, tiled=True)
    o_rows = o_rows.reshape(n_tp, cols, q_cols)

    inv_freq = 500000.0 ** (-(jnp.arange(HEAD // 2, dtype=jnp.float32) * 2.0) / HEAD)
    positions = (shard * rows + jnp.arange(rows, dtype=jnp.int32)).astype(jnp.float32)
    angles = positions[:, None] * inv_freq[None, :]
    cos_part, sin_part = jnp.cos(angles), jnp.sin(angles)
    cos_part = jnp.concatenate([cos_part, cos_part], axis=1)
    sin_part = jnp.concatenate([-sin_part, sin_part], axis=1)
    docs = doc_ids.astype(jnp.float32) + 1.0
    docs_rows = jnp.broadcast_to(docs[None].astype(jnp.bfloat16), (8, rows))

    vmem, hbm, smem = (pl.BlockSpec(memory_space=s) for s in (pltpu.VMEM, pl.ANY, pltpu.SMEM))
    tile, normed = pl.pallas_call(
        kv_kernel,
        out_shape=(
            jax.ShapeDtypeStruct((rows + 8, 2 * kv_cols), jnp.bfloat16),
            jax.ShapeDtypeStruct((rows, n_tp * cols), jnp.bfloat16),
        ),
        in_specs=[smem, vmem, vmem, vmem, vmem] + [hbm] * 8,
        scratch_shapes=[
            pltpu.VMEM((n_tp * cols, 2 * kv_cols), jnp.bfloat16),
            pltpu.SemaphoreType.DMA((1,)),
        ],
        name="kv_projection",
    )(where, whole, docs_rows, cos_part, sin_part, *pieces)
    q_rot = pl.pallas_call(
        q_kernel,
        out_shape=jax.ShapeDtypeStruct((group, rows, HEAD), jnp.bfloat16),
        in_specs=[smem, vmem, vmem, vmem] + [hbm] * 8,
        scratch_shapes=[
            pltpu.VMEM((n_tp * cols, q_cols), jnp.bfloat16),
            pltpu.SemaphoreType.DMA((1,)),
        ],
        cost_estimate=pl.CostEstimate(
            flops=2 * rows * n_tp * cols * q_cols, bytes_accessed=2 * n_tp * cols * (q_cols + rows), transcendentals=0
        ),
        name="q_projection",
    )(where, normed, cos_part, sin_part, *pieces)

    back_1 = lax.ppermute(tile, ("zh", "y"), line(8, 1))
    back_2 = lax.ppermute(tile, ("zh", "y", "tp"), two_back())
    moved = lax.ppermute(back_2, ("zh", "y", "tp"), settle())
    back_2 = jnp.where((zh == 1) & (y < 2), moved, back_2)
    back_1, back_2, q_rot = lax.optimization_barrier((back_1, back_2, q_rot))
    mine = []
    for step in range(1, 4):
        two = jnp.stack([back_1, jnp.where(x + step < 4, tile, back_2)])
        mine.append(lax.ppermute(two, "x", ring(4, step)))
    sent = mine + [jnp.stack([back_1, jnp.where(core == 0, tile, back_2)])]
    other = lax.ppermute(jnp.concatenate(sent), "core", swap)
    mine = jnp.concatenate(mine + [jnp.stack([back_1, tile])])

    attended = pl.pallas_call(
        attention_kernel,
        out_shape=jax.ShapeDtypeStruct((rows, q_cols), jnp.bfloat16),
        in_specs=[vmem] * 4,
        scratch_shapes=[pltpu.VMEM((group * rows, 16 * rows), jnp.float32)],
        name="attention",
    )(q_rot, docs[:, None], mine, other)

    order = (jnp.array(FOLDED, jnp.int32) + 4 * zh) % 8
    partial_terms = pl.pallas_call(
        out_kernel,
        out_shape=jax.ShapeDtypeStruct((n_tp, rows, cols), jnp.bfloat16),
        grid_spec=pltpu.PrefetchScalarGridSpec(
            num_scalar_prefetch=1,
            grid=(n_tp,),
            in_specs=[
                pl.BlockSpec((rows, q_cols), lambda m, order: (0, 0)),
                pl.BlockSpec((1, cols, q_cols), lambda m, order: (order[m], 0, 0)),
            ],
            out_specs=pl.BlockSpec((1, rows, cols), lambda m, order: (m, 0, 0)),
        ),
        name="out_projection",
    )(order, attended, o_rows)
    return lax.psum_scatter(
        partial_terms.reshape(n_tp * rows, cols),
        "tp",
        scatter_dimension=0,
        tiled=True,
        axis_index_groups=[FOLDED],
    )


def solution(mesh):
    fine = Mesh(mesh.devices.reshape(2, 4, 4, 2, 8), ("zh", "y", "x", "core", "tp"))
    ctx = ("zh", "y", "x", "core")
    return jax.shard_map(
        local,
        mesh=fine,
        in_specs=(
            P(ctx, "tp"),
            P("tp"),
            P(ctx),
            P(ctx, "tp"),
            P(ctx, "tp"),
            P(ctx, "tp"),
            P("tp", ctx),
        ),
        out_specs=P(ctx, "tp"),
        check_vma=False,
    )
```

```python
import jax
import jax.numpy as jnp
from jax import lax
from jax.experimental import pallas as pl
from jax.experimental.pallas import tpu as pltpu
from jax.sharding import Mesh, PartitionSpec as P


HEAD = 128
PLANE = ("y", "x", "core")
SC_ROWS = 160


def line(size, step):
    return [(i, i + step) for i in range(size) if 0 <= i + step < size]


def ring(size, step):
    return [(i, (i + step) % size) for i in range(size)]


def plane_route(step, first):
    route = []
    for y in range(4):
        for x in range(4):
            for core in range(2):
                if (core == 0) == first:
                    to = (y * 4 + (x + step) % 4) * 2 + core
                else:
                    to = ((y + step) % 4 * 4 + x) * 2 + core
                route.append(((y * 4 + x) * 2 + core, to))
    return route


def block_rows(where, core, e, d, z):
    zh, y, x = where[0], where[1], where[2]
    far, near = (4 - e) % 4, (4 - d) % 4
    at_y = (y + jnp.where(core == 0, far, near)) % 4
    at_x = (x + jnp.where(core == 0, near, far)) % 4
    at_zh = jnp.where(zh == z, 0, 1)
    return pl.multiple_of((((at_zh * 4 + at_y) * 4 + at_x) * 2 + core) * 64, 64)


def load_weights(where, pieces, buffer, sem, first_col):
    cols = buffer.shape[1]
    copies = []
    for n, piece in enumerate(pieces):
        core = jnp.where(n < 4, where[3], 1 - where[3])
        for d in range(4):
            for z in range(2):
                rows = block_rows(where, core, n % 4, d, z)
                copies.append(
                    pltpu.make_async_copy(
                        piece.at[d, z, :, pl.ds(first_col, cols)], buffer.at[pl.ds(rows, 64)], sem.at[0]
                    )
                )
    for copy in copies:
        copy.start()
    return copies


def turn(values, cos_ref, sin_ref):
    return values * cos_ref[...] + pltpu.roll(values, HEAD // 2, 1) * sin_ref[...]


def kv_kernel(where, x_ref, docs_ref, cos_ref, sin_ref, *rest):
    pieces, (tile_ref, normed_ref, buffer, sem) = rest[:8], rest[8:]
    copies = load_weights(where, pieces, buffer, sem, 512)
    n_tp, _, cols = x_ref.shape
    rows = normed_ref.shape[0]
    square = jnp.zeros((rows, cols), jnp.float32)
    for j in range(n_tp):
        block = x_ref[j, :rows].astype(jnp.float32)
        square = square + block * block
    scale = lax.rsqrt(jnp.sum(square, axis=1, keepdims=True) / (n_tp * cols) + 1e-05)
    for j in range(n_tp):
        block = x_ref[j, :rows].astype(jnp.float32)
        gain = x_ref[j, pl.ds(rows, 1)].astype(jnp.float32)
        normed_ref[:, j * cols : (j + 1) * cols] = (block * scale * gain).astype(jnp.bfloat16)
    for copy in copies:
        copy.wait()
    out = jnp.dot(normed_ref[...], buffer[...], preferred_element_type=jnp.float32)
    tile_ref[:rows, :HEAD] = turn(out[:, :HEAD], cos_ref, sin_ref).astype(jnp.bfloat16)
    tile_ref[:rows, HEAD:] = out[:, HEAD:].astype(jnp.bfloat16)
    tile_ref[rows:, :] = docs_ref[...]


def q_kernel(where, normed_ref, cos_ref, sin_ref, *rest):
    pieces, (q_ref, buffer, sem) = rest[:8], rest[8:]
    copies = load_weights(where, pieces, buffer, sem, 0)
    for copy in copies:
        copy.wait()
    out = jnp.dot(normed_ref[...], buffer[...], preferred_element_type=jnp.float32)
    factor = 1.4426950408889634 / HEAD**0.5
    for g in range(q_ref.shape[0]):
        head = turn(out[:, g * HEAD : (g + 1) * HEAD], cos_ref, sin_ref)
        q_ref[g] = (head * factor).astype(jnp.bfloat16)


def attention_kernel(q_ref, docs_ref, mine_ref, other_ref, out_ref, scores):
    group, rows, head = q_ref.shape
    q_docs = docs_ref[...]
    ones = jnp.ones((8, rows, head), jnp.bfloat16)
    for g in range(group):
        at = slice(g * rows, (g + 1) * rows)
        top = None
        for n in range(16):
            ref, s = (mine_ref, n) if n < 8 else (other_ref, n - 8)
            part = lax.dot_general(
                q_ref[g],
                ref[s, :rows, :head],
                (((1,), (1,)), ((), ())),
                preferred_element_type=jnp.float32,
            )
            allowed = ref[s, pl.ds(rows, 1), :].astype(jnp.float32) == q_docs
            if n == 7:
                q_at = lax.broadcasted_iota(jnp.int32, (rows, rows), 0)
                k_at = lax.broadcasted_iota(jnp.int32, (rows, rows), 1)
                allowed = allowed & (k_at <= q_at)
            part = jnp.where(allowed, part, -1e30)
            scores[at, n * rows : (n + 1) * rows] = part
            most = jnp.maximum(part[:, :head], part[:, head:])
            top = most if top is None else jnp.maximum(top, most)
        top = jnp.max(top, axis=1, keepdims=True)
        expw = jnp.exp2(scores[at, :] - top).astype(jnp.bfloat16)
        summed = jnp.zeros((rows, 2 * head), jnp.float32)
        for n, ref in enumerate((mine_ref, other_ref)):
            values = jnp.concatenate([ref[:, :rows, head:], ones], axis=2)
            values = values.reshape(8 * rows, 2 * head)
            summed = summed + jnp.dot(
                expw[:, n * 8 * rows : (n + 1) * 8 * rows], values, preferred_element_type=jnp.float32
            )
        out_ref[:, g * head : (g + 1) * head] = (summed[:, :head] / summed[:, head:]).astype(
            jnp.bfloat16
        )


def out_kernel(info, a_ref, o_ref, core_ref, sent_ref):
    step = pl.program_id(0)
    for j in range(o_ref.shape[0]):
        part = lax.dot_general(
            a_ref[...], o_ref[j], (((1,), (1,)), ((), ())), preferred_element_type=jnp.float32
        ).astype(jnp.bfloat16)
        core_ref[j] = part[:SC_ROWS]
        which = jnp.where(info[1] == j % 2, 0, 1)
        sent_ref[which, step * 2 + j // 2] = part[SC_ROWS:]


def local(tokens, norm_gain, doc_ids, q_weight, k_weight, v_weight, o_weight):
    rows, cols = tokens.shape
    n_tp = lax.axis_size("tp")
    q_cols = q_weight.shape[1]
    kv_cols = k_weight.shape[1]
    group = q_cols // HEAD
    tp = lax.axis_index("tp")
    zh, y, x, core = (lax.axis_index(a) for a in ("zh", "y", "x", "core"))
    shard = ((zh * 4 + y) * 4 + x) * 2 + core
    where = jnp.stack([zh, y, x, core]).astype(jnp.int32)
    swap = [(0, 1), (1, 0)]

    block = jnp.concatenate([tokens, jnp.broadcast_to(norm_gain[None], (8, cols))], axis=0)
    whole = lax.all_gather(block, "tp", axis=0, tiled=False)

    weight = jnp.concatenate([q_weight, k_weight, v_weight], axis=1)
    away = lax.ppermute(weight, "zh", swap)
    pair = jnp.stack([weight, away])
    near = [pair] + [lax.ppermute(pair, PLANE, plane_route(d, True)) for d in range(1, 4)]
    near = jnp.stack(near)
    pieces = [near] + [lax.ppermute(near, PLANE, plane_route(e, False)) for e in range(1, 4)]

    o_block = o_weight.T
    o_away = lax.ppermute(o_block, "zh", swap)
    o_pair = jnp.stack([o_block, o_away])
    pieces = pieces + [lax.ppermute(piece, "core", swap) for piece in pieces]
    o_rows = lax.all_gather(o_pair, PLANE, axis=1, tiled=True)
    o_rows = o_rows.reshape(n_tp, cols, q_cols)

    inv_freq = 500000.0 ** (-(jnp.arange(HEAD // 2, dtype=jnp.float32) * 2.0) / HEAD)
    positions = (shard * rows + jnp.arange(rows, dtype=jnp.int32)).astype(jnp.float32)
    angles = positions[:, None] * inv_freq[None, :]
    cos_part, sin_part = jnp.cos(angles), jnp.sin(angles)
    cos_part = jnp.concatenate([cos_part, cos_part], axis=1)
    sin_part = jnp.concatenate([-sin_part, sin_part], axis=1)
    docs = doc_ids.astype(jnp.float32) + 1.0
    docs_rows = jnp.broadcast_to(docs[None].astype(jnp.bfloat16), (8, rows))

    vmem, hbm, smem = (pl.BlockSpec(memory_space=s) for s in (pltpu.VMEM, pl.ANY, pltpu.SMEM))
    tile, normed = pl.pallas_call(
        kv_kernel,
        out_shape=(
            jax.ShapeDtypeStruct((rows + 8, 2 * kv_cols), jnp.bfloat16),
            jax.ShapeDtypeStruct((rows, n_tp * cols), jnp.bfloat16),
        ),
        in_specs=[smem, vmem, vmem, vmem, vmem] + [hbm] * 8,
        scratch_shapes=[
            pltpu.VMEM((n_tp * cols, 2 * kv_cols), jnp.bfloat16),
            pltpu.SemaphoreType.DMA((1,)),
        ],
        name="kv_projection",
    )(where, whole, docs_rows, cos_part, sin_part, *pieces)
    q_rot = pl.pallas_call(
        q_kernel,
        out_shape=jax.ShapeDtypeStruct((group, rows, HEAD), jnp.bfloat16),
        in_specs=[smem, vmem, vmem, vmem] + [hbm] * 8,
        scratch_shapes=[
            pltpu.VMEM((n_tp * cols, q_cols), jnp.bfloat16),
            pltpu.SemaphoreType.DMA((1,)),
        ],
        cost_estimate=pl.CostEstimate(
            flops=2 * rows * n_tp * cols * q_cols, bytes_accessed=2 * n_tp * cols * (q_cols + rows), transcendentals=0
        ),
        name="q_projection",
    )(where, normed, cos_part, sin_part, *pieces)

    back_1 = lax.ppermute(tile, ("zh", "y"), line(8, 1))
    back_2 = lax.ppermute(tile, ("zh", "y"), line(8, 2))
    back_1, back_2, q_rot = lax.optimization_barrier((back_1, back_2, q_rot))
    mine = []
    for step in range(1, 4):
        two = jnp.stack([back_1, jnp.where(x + step < 4, tile, back_2)])
        mine.append(lax.ppermute(two, "x", ring(4, step)))
    sent = mine + [jnp.stack([back_1, jnp.where(core == 0, tile, back_2)])]
    other = lax.ppermute(jnp.concatenate(sent), "core", swap)
    mine = jnp.concatenate(mine + [jnp.stack([back_1, tile])])

    attended = pl.pallas_call(
        attention_kernel,
        out_shape=jax.ShapeDtypeStruct((rows, q_cols), jnp.bfloat16),
        in_specs=[vmem] * 4,
        scratch_shapes=[pltpu.VMEM((group * rows, 16 * rows), jnp.float32)],
        name="attention",
    )(q_rot, docs[:, None], mine, other)

    parity, place = tp % 2, tp // 2
    late = rows - SC_ROWS
    half = n_tp // 2
    for_core, sent = pl.pallas_call(
        out_kernel,
        out_shape=(
            jax.ShapeDtypeStruct((n_tp, SC_ROWS, cols), jnp.bfloat16),
            jax.ShapeDtypeStruct((2, half, late, cols), jnp.bfloat16),
        ),
        grid_spec=pltpu.PrefetchScalarGridSpec(
            num_scalar_prefetch=1,
            grid=(2,),
            in_specs=[
                pl.BlockSpec((rows, q_cols), lambda i, info: (0, 0)),
                pl.BlockSpec((half, cols, q_cols), lambda i, info: ((i + info[0]) % 2, 0, 0)),
            ],
            out_specs=(
                pl.BlockSpec((half, SC_ROWS, cols), lambda i, info: (i, 0, 0)),
                pl.BlockSpec((2, half, late, cols), lambda i, info: (0, 0, 0, 0)),
            ),
        ),
        name="out_projection",
    )(jnp.stack([zh, parity]).astype(jnp.int32), attended, o_rows)
    first_rows = lax.psum_scatter(
        for_core.reshape(n_tp * SC_ROWS, cols), "tp", scatter_dimension=0, tiled=True
    )
    theirs = lax.ppermute(sent[1], "tp", [(i, i ^ 1) for i in range(8)])
    ours = (sent[0].astype(jnp.float32) + theirs.astype(jnp.float32)).astype(jnp.bfloat16)
    last_rows = lax.dynamic_index_in_dim(ours, place, 0, keepdims=False).astype(jnp.float32)
    for step in range(1, 4):
        piece = lax.dynamic_index_in_dim(ours, (place + step) % 4, 0, keepdims=False)
        route = [(i, 2 * ((i // 2 + step) % 4) + i % 2) for i in range(8)]
        last_rows = last_rows + lax.ppermute(piece, "tp", route).astype(jnp.float32)
    return jnp.concatenate([first_rows, last_rows.astype(jnp.bfloat16)], axis=0)


def solution(mesh):
    fine = Mesh(mesh.devices.reshape(2, 4, 4, 2, 8), ("zh", "y", "x", "core", "tp"))
    ctx = ("zh", "y", "x", "core")
    return jax.shard_map(
        local,
        mesh=fine,
        in_specs=(
            P(ctx, "tp"),
            P("tp"),
            P(ctx),
            P(ctx, "tp"),
            P(ctx, "tp"),
            P(ctx, "tp"),
            P("tp", ctx),
        ),
        out_specs=P(ctx, "tp"),
        check_vma=False,
    )
```

```python
import jax
import jax.numpy as jnp
from jax import lax
from jax.experimental import pallas as pl
from jax.experimental.pallas import tpu as pltpu
from jax.sharding import Mesh, PartitionSpec as P


HEAD = 128
PLANE = ("y", "x", "core")


def line(size, step):
    return [(i, i + step) for i in range(size) if 0 <= i + step < size]


def ring(size, step):
    return [(i, (i + step) % size) for i in range(size)]


def plane_route(step, first):
    route = []
    for y in range(4):
        for x in range(4):
            for core in range(2):
                if (core == 0) == first:
                    to = (y * 4 + (x + step) % 4) * 2 + core
                else:
                    to = ((y + step) % 4 * 4 + x) * 2 + core
                route.append(((y * 4 + x) * 2 + core, to))
    return route


def block_rows(where, core, e, d, z):
    zh, y, x = where[0], where[1], where[2]
    far, near = (4 - e) % 4, (4 - d) % 4
    at_y = (y + jnp.where(core == 0, far, near)) % 4
    at_x = (x + jnp.where(core == 0, near, far)) % 4
    at_zh = jnp.where(zh == z, 0, 1)
    return pl.multiple_of((((at_zh * 4 + at_y) * 4 + at_x) * 2 + core) * 64, 64)


def load_weights(where, pieces, buffer, sem, first_col):
    cols = buffer.shape[1]
    copies = []
    for n, piece in enumerate(pieces):
        core = jnp.where(n < 4, where[3], 1 - where[3])
        for d in range(4):
            for z in range(2):
                rows = block_rows(where, core, n % 4, d, z)
                copies.append(
                    pltpu.make_async_copy(
                        piece.at[d, z, :, pl.ds(first_col, cols)], buffer.at[pl.ds(rows, 64)], sem.at[0]
                    )
                )
    for copy in copies:
        copy.start()
    return copies


def turn(values, cos_ref, sin_ref):
    return values * cos_ref[...] + pltpu.roll(values, HEAD // 2, 1) * sin_ref[...]


def kv_kernel(where, x_ref, docs_ref, cos_ref, sin_ref, *rest):
    pieces, (tile_ref, normed_ref, buffer, sem) = rest[:8], rest[8:]
    copies = load_weights(where, pieces, buffer, sem, 512)
    n_tp, _, cols = x_ref.shape
    rows = normed_ref.shape[0]
    square = jnp.zeros((rows, cols), jnp.float32)
    for j in range(n_tp):
        block = x_ref[j, :rows].astype(jnp.float32)
        square = square + block * block
    scale = lax.rsqrt(jnp.sum(square, axis=1, keepdims=True) / (n_tp * cols) + 1e-05)
    for j in range(n_tp):
        block = x_ref[j, :rows].astype(jnp.float32)
        gain = x_ref[j, pl.ds(rows, 1)].astype(jnp.float32)
        normed_ref[:, j * cols : (j + 1) * cols] = (block * scale * gain).astype(jnp.bfloat16)
    for copy in copies:
        copy.wait()
    out = jnp.dot(normed_ref[...], buffer[...], preferred_element_type=jnp.float32)
    tile_ref[:rows, :HEAD] = turn(out[:, :HEAD], cos_ref, sin_ref).astype(jnp.bfloat16)
    tile_ref[:rows, HEAD:] = out[:, HEAD:].astype(jnp.bfloat16)
    tile_ref[rows:, :] = docs_ref[...]


def q_kernel(where, normed_ref, cos_ref, sin_ref, *rest):
    pieces, (q_ref, buffer, sem) = rest[:8], rest[8:]
    copies = load_weights(where, pieces, buffer, sem, 0)
    for copy in copies:
        copy.wait()
    out = jnp.dot(normed_ref[...], buffer[...], preferred_element_type=jnp.float32)
    factor = 1.4426950408889634 / HEAD**0.5
    for g in range(q_ref.shape[0]):
        head = turn(out[:, g * HEAD : (g + 1) * HEAD], cos_ref, sin_ref)
        q_ref[g] = (head * factor).astype(jnp.bfloat16)


def attention_kernel(q_ref, docs_ref, mine_ref, other_ref, out_ref, scores):
    group, rows, head = q_ref.shape
    q_docs = docs_ref[...]
    ones = jnp.ones((8, rows, head), jnp.bfloat16)
    for g in range(group):
        at = slice(g * rows, (g + 1) * rows)
        top = None
        for n in range(16):
            ref, s = (mine_ref, n) if n < 8 else (other_ref, n - 8)
            part = lax.dot_general(
                q_ref[g],
                ref[s, :rows, :head],
                (((1,), (1,)), ((), ())),
                preferred_element_type=jnp.float32,
            )
            allowed = ref[s, pl.ds(rows, 1), :].astype(jnp.float32) == q_docs
            if n == 7:
                q_at = lax.broadcasted_iota(jnp.int32, (rows, rows), 0)
                k_at = lax.broadcasted_iota(jnp.int32, (rows, rows), 1)
                allowed = allowed & (k_at <= q_at)
            part = jnp.where(allowed, part, -1e30)
            scores[at, n * rows : (n + 1) * rows] = part
            most = jnp.maximum(part[:, :head], part[:, head:])
            top = most if top is None else jnp.maximum(top, most)
        top = jnp.max(top, axis=1, keepdims=True)
        expw = jnp.exp2(scores[at, :] - top).astype(jnp.bfloat16)
        summed = jnp.zeros((rows, 2 * head), jnp.float32)
        for n, ref in enumerate((mine_ref, other_ref)):
            values = jnp.concatenate([ref[:, :rows, head:], ones], axis=2)
            values = values.reshape(8 * rows, 2 * head)
            summed = summed + jnp.dot(
                expw[:, n * 8 * rows : (n + 1) * 8 * rows], values, preferred_element_type=jnp.float32
            )
        out_ref[:, g * head : (g + 1) * head] = (summed[:, :head] / summed[:, head:]).astype(
            jnp.bfloat16
        )


def out_kernel(zh, a_ref, o_ref, out_ref):
    del zh
    for j in range(o_ref.shape[0]):
        out_ref[j] = lax.dot_general(
            a_ref[...], o_ref[j], (((1,), (1,)), ((), ())), preferred_element_type=jnp.float32
        ).astype(jnp.bfloat16)


def local(tokens, norm_gain, doc_ids, q_weight, k_weight, v_weight, o_weight):
    rows, cols = tokens.shape
    n_tp = lax.axis_size("tp")
    q_cols = q_weight.shape[1]
    kv_cols = k_weight.shape[1]
    group = q_cols // HEAD
    zh, y, x, core = (lax.axis_index(a) for a in ("zh", "y", "x", "core"))
    shard = ((zh * 4 + y) * 4 + x) * 2 + core
    where = jnp.stack([zh, y, x, core]).astype(jnp.int32)
    swap = [(0, 1), (1, 0)]

    block = jnp.concatenate([tokens, jnp.broadcast_to(norm_gain[None], (8, cols))], axis=0)
    whole = lax.all_gather(block, "tp", axis=0, tiled=False)

    weight = jnp.concatenate([q_weight, k_weight, v_weight], axis=1)
    away = lax.ppermute(weight, "zh", swap)
    pair = jnp.stack([weight, away])
    near = [pair] + [lax.ppermute(pair, PLANE, plane_route(d, True)) for d in range(1, 4)]
    near = jnp.stack(near)
    pieces = [near] + [lax.ppermute(near, PLANE, plane_route(e, False)) for e in range(1, 4)]

    o_block = o_weight.T
    o_away = lax.ppermute(o_block, "zh", swap)
    o_pair = jnp.stack([o_block, o_away])
    pieces = pieces + [lax.ppermute(piece, "core", swap) for piece in pieces]
    o_rows = lax.all_gather(o_pair, PLANE, axis=1, tiled=True)
    o_rows = o_rows.reshape(n_tp, cols, q_cols)

    inv_freq = 500000.0 ** (-(jnp.arange(HEAD // 2, dtype=jnp.float32) * 2.0) / HEAD)
    positions = (shard * rows + jnp.arange(rows, dtype=jnp.int32)).astype(jnp.float32)
    angles = positions[:, None] * inv_freq[None, :]
    cos_part, sin_part = jnp.cos(angles), jnp.sin(angles)
    cos_part = jnp.concatenate([cos_part, cos_part], axis=1)
    sin_part = jnp.concatenate([-sin_part, sin_part], axis=1)
    docs = doc_ids.astype(jnp.float32) + 1.0
    docs_rows = jnp.broadcast_to(docs[None].astype(jnp.bfloat16), (8, rows))

    vmem, hbm, smem = (pl.BlockSpec(memory_space=s) for s in (pltpu.VMEM, pl.ANY, pltpu.SMEM))
    tile, normed = pl.pallas_call(
        kv_kernel,
        out_shape=(
            jax.ShapeDtypeStruct((rows + 8, 2 * kv_cols), jnp.bfloat16),
            jax.ShapeDtypeStruct((rows, n_tp * cols), jnp.bfloat16),
        ),
        in_specs=[smem, vmem, vmem, vmem, vmem] + [hbm] * 8,
        scratch_shapes=[
            pltpu.VMEM((n_tp * cols, 2 * kv_cols), jnp.bfloat16),
            pltpu.SemaphoreType.DMA((1,)),
        ],
        name="kv_projection",
    )(where, whole, docs_rows, cos_part, sin_part, *pieces)
    q_rot = pl.pallas_call(
        q_kernel,
        out_shape=jax.ShapeDtypeStruct((group, rows, HEAD), jnp.bfloat16),
        in_specs=[smem, vmem, vmem, vmem] + [hbm] * 8,
        scratch_shapes=[
            pltpu.VMEM((n_tp * cols, q_cols), jnp.bfloat16),
            pltpu.SemaphoreType.DMA((1,)),
        ],
        cost_estimate=pl.CostEstimate(
            flops=2 * rows * n_tp * cols * q_cols, bytes_accessed=2 * n_tp * cols * (q_cols + rows), transcendentals=0
        ),
        name="q_projection",
    )(where, normed, cos_part, sin_part, *pieces)

    back_1 = lax.ppermute(tile, ("zh", "y"), line(8, 1))
    back_2 = lax.ppermute(tile, ("zh", "y"), line(8, 2))
    back_1, back_2, q_rot = lax.optimization_barrier((back_1, back_2, q_rot))
    mine = []
    for step in range(1, 4):
        two = jnp.stack([back_1, jnp.where(x + step < 4, tile, back_2)])
        mine.append(lax.ppermute(two, "x", ring(4, step)))
    sent = mine + [jnp.stack([back_1, jnp.where(core == 0, tile, back_2)])]
    other = lax.ppermute(jnp.concatenate(sent), "core", swap)
    mine = jnp.concatenate(mine + [jnp.stack([back_1, tile])])

    attended = pl.pallas_call(
        attention_kernel,
        out_shape=jax.ShapeDtypeStruct((rows, q_cols), jnp.bfloat16),
        in_specs=[vmem] * 4,
        scratch_shapes=[pltpu.VMEM((group * rows, 16 * rows), jnp.float32)],
        name="attention",
    )(q_rot, docs[:, None], mine, other)

    half = n_tp // 2
    partial_terms = pl.pallas_call(
        out_kernel,
        out_shape=jax.ShapeDtypeStruct((n_tp, rows, cols), jnp.bfloat16),
        grid_spec=pltpu.PrefetchScalarGridSpec(
            num_scalar_prefetch=1,
            grid=(2,),
            in_specs=[
                pl.BlockSpec((rows, q_cols), lambda i, zh: (0, 0)),
                pl.BlockSpec((half, cols, q_cols), lambda i, zh: ((i + zh[0]) % 2, 0, 0)),
            ],
            out_specs=pl.BlockSpec((half, rows, cols), lambda i, zh: (i, 0, 0)),
        ),
        name="out_projection",
    )(where[:1], attended, o_rows)
    return lax.psum_scatter(
        partial_terms.reshape(n_tp * rows, cols), "tp", scatter_dimension=0, tiled=True
    )


def solution(mesh):
    fine = Mesh(mesh.devices.reshape(2, 4, 4, 2, 8), ("zh", "y", "x", "core", "tp"))
    ctx = ("zh", "y", "x", "core")
    return jax.shard_map(
        local,
        mesh=fine,
        in_specs=(
            P(ctx, "tp"),
            P("tp"),
            P(ctx),
            P(ctx, "tp"),
            P(ctx, "tp"),
            P(ctx, "tp"),
            P("tp", ctx),
        ),
        out_specs=P(ctx, "tp"),
        check_vma=False,
    )
```

```python
import jax
import jax.numpy as jnp
from jax import lax
from jax.experimental import pallas as pl
from jax.experimental.pallas import tpu as pltpu
from jax.sharding import Mesh, PartitionSpec as P


HEAD = 128
PLANE = ("y", "x", "core")
FOLDED = [0, 2, 4, 6, 7, 5, 3, 1]


def line(size, step):
    return [(i, i + step) for i in range(size) if 0 <= i + step < size]


def ring(size, step):
    return [(i, (i + step) % size) for i in range(size)]


def plane_route(step, first):
    route = []
    for y in range(4):
        for x in range(4):
            for core in range(2):
                if (core == 0) == first:
                    to = (y * 4 + (x + step) % 4) * 2 + core
                else:
                    to = ((y + step) % 4 * 4 + x) * 2 + core
                route.append(((y * 4 + x) * 2 + core, to))
    return route


def block_rows(where, core, e, d, z):
    zh, y, x = where[0], where[1], where[2]
    far, near = (4 - e) % 4, (4 - d) % 4
    at_y = (y + jnp.where(core == 0, far, near)) % 4
    at_x = (x + jnp.where(core == 0, near, far)) % 4
    at_zh = jnp.where(zh == z, 0, 1)
    return pl.multiple_of((((at_zh * 4 + at_y) * 4 + at_x) * 2 + core) * 64, 64)


def load_weights(where, pieces, buffer, sem, first_col):
    cols = buffer.shape[1]
    copies = []
    for n, piece in enumerate(pieces):
        core = jnp.where(n % 8 < 4, where[3], 1 - where[3])
        for d in range(4):
            rows = block_rows(where, core, n % 4, d, n // 8)
            copies.append(
                pltpu.make_async_copy(
                    piece.at[d, :, pl.ds(first_col, cols)], buffer.at[pl.ds(rows, 64)], sem.at[0]
                )
            )
    for copy in copies:
        copy.start()
    return copies


def turn(values, cos_ref, sin_ref):
    return values * cos_ref[...] + pltpu.roll(values, HEAD // 2, 1) * sin_ref[...]


def kv_kernel(where, x_ref, docs_ref, cos_ref, sin_ref, *rest):
    pieces, (tile_ref, normed_ref, buffer, sem) = rest[:16], rest[16:]
    copies = load_weights(where, pieces, buffer, sem, 512)
    n_tp, _, cols = x_ref.shape
    rows = normed_ref.shape[0]
    square = jnp.zeros((rows, cols), jnp.float32)
    for j in range(n_tp):
        block = x_ref[j, :rows].astype(jnp.float32)
        square = square + block * block
    scale = lax.rsqrt(jnp.sum(square, axis=1, keepdims=True) / (n_tp * cols) + 1e-05)
    for j in range(n_tp):
        block = x_ref[j, :rows].astype(jnp.float32)
        gain = x_ref[j, pl.ds(rows, 1)].astype(jnp.float32)
        at = FOLDED[j] * cols
        normed_ref[:, at : at + cols] = (block * scale * gain).astype(jnp.bfloat16)
    for copy in copies:
        copy.wait()
    out = jnp.dot(normed_ref[...], buffer[...], preferred_element_type=jnp.float32)
    tile_ref[:rows, :HEAD] = turn(out[:, :HEAD], cos_ref, sin_ref).astype(jnp.bfloat16)
    tile_ref[:rows, HEAD:] = out[:, HEAD:].astype(jnp.bfloat16)
    tile_ref[rows:, :] = docs_ref[...]


def q_kernel(where, normed_ref, cos_ref, sin_ref, *rest):
    pieces, (q_ref, buffer, sem) = rest[:16], rest[16:]
    copies = load_weights(where, pieces, buffer, sem, 0)
    for copy in copies:
        copy.wait()
    out = jnp.dot(normed_ref[...], buffer[...], preferred_element_type=jnp.float32)
    factor = 1.4426950408889634 / HEAD**0.5
    for g in range(q_ref.shape[0]):
        head = turn(out[:, g * HEAD : (g + 1) * HEAD], cos_ref, sin_ref)
        q_ref[g] = (head * factor).astype(jnp.bfloat16)


def attention_kernel(q_ref, docs_ref, mine_ref, other_ref, out_ref, scores):
    group, rows, head = q_ref.shape
    q_docs = docs_ref[...]
    ones = jnp.ones((8, rows, head), jnp.bfloat16)
    for g in range(group):
        at = slice(g * rows, (g + 1) * rows)
        top = None
        for n in range(16):
            ref, s = (mine_ref, n) if n < 8 else (other_ref, n - 8)
            part = lax.dot_general(
                q_ref[g],
                ref[s, :rows, :head],
                (((1,), (1,)), ((), ())),
                preferred_element_type=jnp.float32,
            )
            allowed = ref[s, pl.ds(rows, 1), :].astype(jnp.float32) == q_docs
            if n == 7:
                q_at = lax.broadcasted_iota(jnp.int32, (rows, rows), 0)
                k_at = lax.broadcasted_iota(jnp.int32, (rows, rows), 1)
                allowed = allowed & (k_at <= q_at)
            part = jnp.where(allowed, part, -1e30)
            scores[at, n * rows : (n + 1) * rows] = part
            most = jnp.maximum(part[:, :head], part[:, head:])
            top = most if top is None else jnp.maximum(top, most)
        top = jnp.max(top, axis=1, keepdims=True)
        expw = jnp.exp2(scores[at, :] - top).astype(jnp.bfloat16)
        summed = jnp.zeros((rows, 2 * head), jnp.float32)
        for n, ref in enumerate((mine_ref, other_ref)):
            values = jnp.concatenate([ref[:, :rows, head:], ones], axis=2)
            values = values.reshape(8 * rows, 2 * head)
            summed = summed + jnp.dot(
                expw[:, n * 8 * rows : (n + 1) * 8 * rows], values, preferred_element_type=jnp.float32
            )
        out_ref[:, g * head : (g + 1) * head] = (summed[:, :head] / summed[:, head:]).astype(
            jnp.bfloat16
        )


def out_kernel(zh, a_ref, o_ref, out_ref):
    for n in range(o_ref.shape[0]):
        block = (jnp.where(pl.program_id(0) == 0, n, 3 - n) + 2 * zh[0]) % 4
        out_ref[n] = lax.dot_general(
            a_ref[...], o_ref[block, 0], (((1,), (1,)), ((), ())), preferred_element_type=jnp.float32
        ).astype(jnp.bfloat16)


def local(tokens, norm_gain, doc_ids, q_weight, k_weight, v_weight, o_weight):
    rows, cols = tokens.shape
    n_tp = lax.axis_size("tp")
    q_cols = q_weight.shape[1]
    kv_cols = k_weight.shape[1]
    group = q_cols // HEAD
    zh, y, x, core = (lax.axis_index(a) for a in ("zh", "y", "x", "core"))
    shard = ((zh * 4 + y) * 4 + x) * 2 + core
    where = jnp.stack([zh, y, x, core]).astype(jnp.int32)
    swap = [(0, 1), (1, 0)]

    block = jnp.concatenate([tokens, jnp.broadcast_to(norm_gain[None], (8, cols))], axis=0)
    whole = lax.all_gather(block, "tp", axis=0, tiled=False, axis_index_groups=[FOLDED])

    def spread(mine):
        near = [mine] + [lax.ppermute(mine, PLANE, plane_route(d, True)) for d in range(1, 4)]
        near = jnp.stack(near)
        far = [near] + [lax.ppermute(near, PLANE, plane_route(e, False)) for e in range(1, 4)]
        return far + [lax.ppermute(piece, "core", swap) for piece in far]

    weight = jnp.concatenate([q_weight, k_weight, v_weight], axis=1)
    away = lax.ppermute(weight, "zh", swap)
    pieces = spread(weight) + spread(away)

    o_block = o_weight.T
    o_away = lax.ppermute(o_block, "zh", swap)
    o_pair = jnp.stack([o_block, o_away])
    o_rows = lax.all_gather(o_pair, PLANE, axis=1, tiled=True)
    o_rows = o_rows.reshape(n_tp, cols, q_cols)

    inv_freq = 500000.0 ** (-(jnp.arange(HEAD // 2, dtype=jnp.float32) * 2.0) / HEAD)
    positions = (shard * rows + jnp.arange(rows, dtype=jnp.int32)).astype(jnp.float32)
    angles = positions[:, None] * inv_freq[None, :]
    cos_part, sin_part = jnp.cos(angles), jnp.sin(angles)
    cos_part = jnp.concatenate([cos_part, cos_part], axis=1)
    sin_part = jnp.concatenate([-sin_part, sin_part], axis=1)
    docs = doc_ids.astype(jnp.float32) + 1.0
    docs_rows = jnp.broadcast_to(docs[None].astype(jnp.bfloat16), (8, rows))

    vmem, hbm, smem = (pl.BlockSpec(memory_space=s) for s in (pltpu.VMEM, pl.ANY, pltpu.SMEM))
    tile, normed = pl.pallas_call(
        kv_kernel,
        out_shape=(
            jax.ShapeDtypeStruct((rows + 8, 2 * kv_cols), jnp.bfloat16),
            jax.ShapeDtypeStruct((rows, n_tp * cols), jnp.bfloat16),
        ),
        in_specs=[smem, vmem, vmem, vmem, vmem] + [hbm] * 16,
        scratch_shapes=[
            pltpu.VMEM((n_tp * cols, 2 * kv_cols), jnp.bfloat16),
            pltpu.SemaphoreType.DMA((1,)),
        ],
        name="kv_projection",
    )(where, whole, docs_rows, cos_part, sin_part, *pieces)
    q_rot = pl.pallas_call(
        q_kernel,
        out_shape=jax.ShapeDtypeStruct((group, rows, HEAD), jnp.bfloat16),
        in_specs=[smem, vmem, vmem, vmem] + [hbm] * 16,
        scratch_shapes=[
            pltpu.VMEM((n_tp * cols, q_cols), jnp.bfloat16),
            pltpu.SemaphoreType.DMA((1,)),
        ],
        cost_estimate=pl.CostEstimate(
            flops=2 * rows * n_tp * cols * q_cols, bytes_accessed=2 * n_tp * cols * (q_cols + rows), transcendentals=0
        ),
        name="q_projection",
    )(where, normed, cos_part, sin_part, *pieces)

    back_1 = lax.ppermute(tile, ("zh", "y"), line(8, 1))
    back_2 = lax.ppermute(tile, ("zh", "y"), line(8, 2))
    back_1, back_2, q_rot = lax.optimization_barrier((back_1, back_2, q_rot))
    mine = []
    for step in range(1, 4):
        two = jnp.stack([back_1, jnp.where(x + step < 4, tile, back_2)])
        mine.append(lax.ppermute(two, "x", ring(4, step)))
    sent = mine + [jnp.stack([back_1, jnp.where(core == 0, tile, back_2)])]
    other = lax.ppermute(jnp.concatenate(sent), "core", swap)
    mine = jnp.concatenate(mine + [jnp.stack([back_1, tile])])

    attended = pl.pallas_call(
        attention_kernel,
        out_shape=jax.ShapeDtypeStruct((rows, q_cols), jnp.bfloat16),
        in_specs=[vmem] * 4,
        scratch_shapes=[pltpu.VMEM((group * rows, 16 * rows), jnp.float32)],
        name="attention",
    )(q_rot, docs[:, None], mine, other)

    half = n_tp // 2
    partial_terms = pl.pallas_call(
        out_kernel,
        out_shape=jax.ShapeDtypeStruct((n_tp, rows, cols), jnp.bfloat16),
        grid_spec=pltpu.PrefetchScalarGridSpec(
            num_scalar_prefetch=1,
            grid=(2,),
            in_specs=[
                pl.BlockSpec((rows, q_cols), lambda i, zh: (0, 0)),
                pl.BlockSpec((half, 1, cols, q_cols), lambda i, zh: (0, i, 0, 0)),
            ],
            out_specs=pl.BlockSpec((half, rows, cols), lambda i, zh: (i, 0, 0)),
        ),
        name="out_projection",
    )(where[:1], attended, o_rows.reshape(half, 2, cols, q_cols))
    return lax.psum_scatter(
        partial_terms.reshape(n_tp * rows, cols),
        "tp",
        scatter_dimension=0,
        tiled=True,
        axis_index_groups=[FOLDED],
    )


def solution(mesh):
    fine = Mesh(mesh.devices.reshape(2, 4, 4, 2, 8), ("zh", "y", "x", "core", "tp"))
    ctx = ("zh", "y", "x", "core")
    return jax.shard_map(
        local,
        mesh=fine,
        in_specs=(
            P(ctx, "tp"),
            P("tp"),
            P(ctx),
            P(ctx, "tp"),
            P(ctx, "tp"),
            P(ctx, "tp"),
            P("tp", ctx),
        ),
        out_specs=P(ctx, "tp"),
        check_vma=False,
    )
```

```python
import jax
import jax.numpy as jnp
from jax import lax
from jax.experimental import pallas as pl
from jax.experimental.pallas import tpu as pltpu
from jax.sharding import Mesh, PartitionSpec as P


HEAD = 128
PLANE = ("y", "x", "core")
FOLDED = [0, 2, 4, 6, 7, 5, 3, 1]


def line(size, step):
    return [(i, i + step) for i in range(size) if 0 <= i + step < size]


def ring(size, step):
    return [(i, (i + step) % size) for i in range(size)]


def plane_route(step, first):
    route = []
    for y in range(4):
        for x in range(4):
            for core in range(2):
                if (core == 0) == first:
                    to = (y * 4 + (x + step) % 4) * 2 + core
                else:
                    to = ((y + step) % 4 * 4 + x) * 2 + core
                route.append(((y * 4 + x) * 2 + core, to))
    return route


def block_rows(where, core, e, d, z):
    zh, y, x = where[0], where[1], where[2]
    far, near = (4 - e) % 4, (4 - d) % 4
    at_y = (y + jnp.where(core == 0, far, near)) % 4
    at_x = (x + jnp.where(core == 0, near, far)) % 4
    at_zh = jnp.where(zh == z, 0, 1)
    return pl.multiple_of((((at_zh * 4 + at_y) * 4 + at_x) * 2 + core) * 64, 64)


def load_weights(where, pieces, buffer, sem, first_col):
    cols = buffer.shape[1]
    copies = []
    for n, piece in enumerate(pieces):
        core = jnp.where(n < 4, where[3], 1 - where[3])
        for d in range(4):
            for z in range(2):
                rows = block_rows(where, core, n % 4, d, z)
                copies.append(
                    pltpu.make_async_copy(
                        piece.at[d, z, :, pl.ds(first_col, cols)], buffer.at[pl.ds(rows, 64)], sem.at[0]
                    )
                )
    for copy in copies:
        copy.start()
    return copies


def turn(values, cos_ref, sin_ref):
    return values * cos_ref[...] + pltpu.roll(values, HEAD // 2, 1) * sin_ref[...]


def kv_kernel(where, x_ref, docs_ref, cos_ref, sin_ref, *rest):
    pieces, (tile_ref, normed_ref, buffer, sem) = rest[:8], rest[8:]
    copies = load_weights(where, pieces, buffer, sem, 512)
    n_tp, _, cols = x_ref.shape
    rows = normed_ref.shape[0]
    square = jnp.zeros((rows, cols), jnp.float32)
    for j in range(n_tp):
        block = x_ref[j, :rows].astype(jnp.float32)
        square = square + block * block
    scale = lax.rsqrt(jnp.sum(square, axis=1, keepdims=True) / (n_tp * cols) + 1e-05)
    for j in range(n_tp):
        block = x_ref[j, :rows].astype(jnp.float32)
        gain = x_ref[j, pl.ds(rows, 1)].astype(jnp.float32)
        at = FOLDED[j] * cols
        normed_ref[:, at : at + cols] = (block * scale * gain).astype(jnp.bfloat16)
    for copy in copies:
        copy.wait()
    out = jnp.dot(normed_ref[...], buffer[...], preferred_element_type=jnp.float32)
    tile_ref[:rows, :HEAD] = turn(out[:, :HEAD], cos_ref, sin_ref).astype(jnp.bfloat16)
    tile_ref[:rows, HEAD:] = out[:, HEAD:].astype(jnp.bfloat16)
    tile_ref[rows:, :] = docs_ref[...]


def q_kernel(where, normed_ref, cos_ref, sin_ref, *rest):
    pieces, (q_ref, buffer, sem) = rest[:8], rest[8:]
    copies = load_weights(where, pieces, buffer, sem, 0)
    for copy in copies:
        copy.wait()
    out = jnp.dot(normed_ref[...], buffer[...], preferred_element_type=jnp.float32)
    factor = 1.4426950408889634 / HEAD**0.5
    for g in range(q_ref.shape[0]):
        head = turn(out[:, g * HEAD : (g + 1) * HEAD], cos_ref, sin_ref)
        q_ref[g] = (head * factor).astype(jnp.bfloat16)


def attention_kernel(q_ref, docs_ref, mine_ref, other_ref, out_ref, scores):
    group, rows, head = q_ref.shape
    q_docs = docs_ref[...]
    ones = jnp.ones((8, rows, head), jnp.bfloat16)
    for g in range(group):
        at = slice(g * rows, (g + 1) * rows)
        top = None
        for n in range(16):
            ref, s = (mine_ref, n) if n < 8 else (other_ref, n - 8)
            part = lax.dot_general(
                q_ref[g],
                ref[s, :rows, :head],
                (((1,), (1,)), ((), ())),
                preferred_element_type=jnp.float32,
            )
            allowed = ref[s, pl.ds(rows, 1), :].astype(jnp.float32) == q_docs
            if n == 7:
                q_at = lax.broadcasted_iota(jnp.int32, (rows, rows), 0)
                k_at = lax.broadcasted_iota(jnp.int32, (rows, rows), 1)
                allowed = allowed & (k_at <= q_at)
            part = jnp.where(allowed, part, -1e30)
            scores[at, n * rows : (n + 1) * rows] = part
            most = jnp.maximum(part[:, :head], part[:, head:])
            top = most if top is None else jnp.maximum(top, most)
        top = jnp.max(top, axis=1, keepdims=True)
        expw = jnp.exp2(scores[at, :] - top).astype(jnp.bfloat16)
        summed = jnp.zeros((rows, 2 * head), jnp.float32)
        for n, ref in enumerate((mine_ref, other_ref)):
            values = jnp.concatenate([ref[:, :rows, head:], ones], axis=2)
            values = values.reshape(8 * rows, 2 * head)
            summed = summed + jnp.dot(
                expw[:, n * 8 * rows : (n + 1) * 8 * rows], values, preferred_element_type=jnp.float32
            )
        out_ref[:, g * head : (g + 1) * head] = (summed[:, :head] / summed[:, head:]).astype(
            jnp.bfloat16
        )


def out_kernel(zh, a_ref, o_ref, out_ref):
    for n in range(o_ref.shape[0]):
        block = (jnp.where(pl.program_id(0) == 0, n, 3 - n) + 2 * zh[0]) % 4
        out_ref[n] = lax.dot_general(
            a_ref[...], o_ref[block, 0], (((1,), (1,)), ((), ())), preferred_element_type=jnp.float32
        ).astype(jnp.bfloat16)


def local(tokens, norm_gain, doc_ids, q_weight, k_weight, v_weight, o_weight):
    rows, cols = tokens.shape
    n_tp = lax.axis_size("tp")
    q_cols = q_weight.shape[1]
    kv_cols = k_weight.shape[1]
    group = q_cols // HEAD
    zh, y, x, core = (lax.axis_index(a) for a in ("zh", "y", "x", "core"))
    shard = ((zh * 4 + y) * 4 + x) * 2 + core
    where = jnp.stack([zh, y, x, core]).astype(jnp.int32)
    swap = [(0, 1), (1, 0)]

    block = jnp.concatenate([tokens, jnp.broadcast_to(norm_gain[None], (8, cols))], axis=0)
    whole = lax.all_gather(block, "tp", axis=0, tiled=False, axis_index_groups=[FOLDED])

    weight = jnp.concatenate([q_weight, k_weight, v_weight], axis=1)
    away = lax.ppermute(weight, "zh", swap)
    pair = jnp.stack([weight, away])
    near = [pair] + [lax.ppermute(pair, PLANE, plane_route(d, True)) for d in range(1, 4)]
    near = jnp.stack(near)
    pieces = [near] + [lax.ppermute(near, PLANE, plane_route(e, False)) for e in range(1, 4)]

    o_block = o_weight.T
    o_away = lax.ppermute(o_block, "zh", swap)
    o_pair = jnp.stack([o_block, o_away])
    pieces = pieces + [lax.ppermute(piece, "core", swap) for piece in pieces]
    o_rows = lax.all_gather(o_pair, PLANE, axis=1, tiled=True)
    o_rows = o_rows.reshape(n_tp, cols, q_cols)

    inv_freq = 500000.0 ** (-(jnp.arange(HEAD // 2, dtype=jnp.float32) * 2.0) / HEAD)
    positions = (shard * rows + jnp.arange(rows, dtype=jnp.int32)).astype(jnp.float32)
    angles = positions[:, None] * inv_freq[None, :]
    cos_part, sin_part = jnp.cos(angles), jnp.sin(angles)
    cos_part = jnp.concatenate([cos_part, cos_part], axis=1)
    sin_part = jnp.concatenate([-sin_part, sin_part], axis=1)
    doc_ids, pieces[4] = lax.optimization_barrier((doc_ids, pieces[4]))
    docs = doc_ids.astype(jnp.float32) + 1.0
    docs_rows = jnp.broadcast_to(docs[None].astype(jnp.bfloat16), (8, rows))

    vmem, hbm, smem = (pl.BlockSpec(memory_space=s) for s in (pltpu.VMEM, pl.ANY, pltpu.SMEM))
    tile, normed = pl.pallas_call(
        kv_kernel,
        out_shape=(
            jax.ShapeDtypeStruct((rows + 8, 2 * kv_cols), jnp.bfloat16),
            jax.ShapeDtypeStruct((rows, n_tp * cols), jnp.bfloat16),
        ),
        in_specs=[smem, vmem, vmem, vmem, vmem] + [hbm] * 8,
        scratch_shapes=[
            pltpu.VMEM((n_tp * cols, 2 * kv_cols), jnp.bfloat16),
            pltpu.SemaphoreType.DMA((1,)),
        ],
        name="kv_projection",
    )(where, whole, docs_rows, cos_part, sin_part, *pieces)
    q_rot = pl.pallas_call(
        q_kernel,
        out_shape=jax.ShapeDtypeStruct((group, rows, HEAD), jnp.bfloat16),
        in_specs=[smem, vmem, vmem, vmem] + [hbm] * 8,
        scratch_shapes=[
            pltpu.VMEM((n_tp * cols, q_cols), jnp.bfloat16),
            pltpu.SemaphoreType.DMA((1,)),
        ],
        cost_estimate=pl.CostEstimate(
            flops=2 * rows * n_tp * cols * q_cols, bytes_accessed=2 * n_tp * cols * (q_cols + rows), transcendentals=0
        ),
        name="q_projection",
    )(where, normed, cos_part, sin_part, *pieces)

    back_1 = lax.ppermute(tile, ("zh", "y"), line(8, 1))
    back_2 = lax.ppermute(tile, ("zh", "y"), line(8, 2))
    back_1, back_2, q_rot = lax.optimization_barrier((back_1, back_2, q_rot))
    mine = []
    for step in range(1, 4):
        two = jnp.stack([back_1, jnp.where(x + step < 4, tile, back_2)])
        mine.append(lax.ppermute(two, "x", ring(4, step)))
    sent = mine + [jnp.stack([back_1, jnp.where(core == 0, tile, back_2)])]
    other = lax.ppermute(jnp.concatenate(sent), "core", swap)
    mine = jnp.concatenate(mine + [jnp.stack([back_1, tile])])

    attended = pl.pallas_call(
        attention_kernel,
        out_shape=jax.ShapeDtypeStruct((rows, q_cols), jnp.bfloat16),
        in_specs=[vmem] * 4,
        scratch_shapes=[pltpu.VMEM((group * rows, 16 * rows), jnp.float32)],
        name="attention",
    )(q_rot, docs[:, None], mine, other)

    half = n_tp // 2
    partial_terms = pl.pallas_call(
        out_kernel,
        out_shape=jax.ShapeDtypeStruct((n_tp, rows, cols), jnp.bfloat16),
        grid_spec=pltpu.PrefetchScalarGridSpec(
            num_scalar_prefetch=1,
            grid=(2,),
            in_specs=[
                pl.BlockSpec((rows, q_cols), lambda i, zh: (0, 0)),
                pl.BlockSpec((half, 1, cols, q_cols), lambda i, zh: (0, i, 0, 0)),
            ],
            out_specs=pl.BlockSpec((half, rows, cols), lambda i, zh: (i, 0, 0)),
        ),
        name="out_projection",
    )(where[:1], attended, o_rows.reshape(half, 2, cols, q_cols))
    return lax.psum_scatter(
        partial_terms.reshape(n_tp * rows, cols),
        "tp",
        scatter_dimension=0,
        tiled=True,
        axis_index_groups=[FOLDED],
    )


def solution(mesh):
    fine = Mesh(mesh.devices.reshape(2, 4, 4, 2, 8), ("zh", "y", "x", "core", "tp"))
    ctx = ("zh", "y", "x", "core")
    return jax.shard_map(
        local,
        mesh=fine,
        in_specs=(
            P(ctx, "tp"),
            P("tp"),
            P(ctx),
            P(ctx, "tp"),
            P(ctx, "tp"),
            P(ctx, "tp"),
            P("tp", ctx),
        ),
        out_specs=P(ctx, "tp"),
        check_vma=False,
    )
```

```python
import jax
import jax.numpy as jnp
from jax import lax
from jax.experimental import pallas as pl
from jax.experimental.pallas import tpu as pltpu
from jax.sharding import Mesh, PartitionSpec as P


HEAD = 128
PLANE = ("y", "x", "core")
FOLDED = [0, 2, 4, 6, 7, 5, 3, 1]


def ring(size, step):
    return [(i, (i + step) % size) for i in range(size)]


def plane_route(step, first):
    route = []
    for y in range(4):
        for x in range(4):
            for core in range(2):
                if (core == 0) == first:
                    to = (y * 4 + (x + step) % 4) * 2 + core
                else:
                    to = ((y + step) % 4 * 4 + x) * 2 + core
                route.append(((y * 4 + x) * 2 + core, to))
    return route


def block_rows(where, core, e, d, z):
    zh, y, x = where[0], where[1], where[2]
    far, near = (4 - e) % 4, (4 - d) % 4
    at_y = (y + jnp.where(core == 0, far, near)) % 4
    at_x = (x + jnp.where(core == 0, near, far)) % 4
    at_zh = jnp.where(zh == z, 0, 1)
    return pl.multiple_of((((at_zh * 4 + at_y) * 4 + at_x) * 2 + core) * 64, 64)


def load_weights(where, pieces, buffer, sem, first_col):
    cols = buffer.shape[1]
    copies = []
    for n, piece in enumerate(pieces):
        core = jnp.where(n < 4, where[3], 1 - where[3])
        for d in range(4):
            for z in range(2):
                rows = block_rows(where, core, n % 4, d, z)
                copies.append(
                    pltpu.make_async_copy(
                        piece.at[d, z, :, pl.ds(first_col, cols)], buffer.at[pl.ds(rows, 64)], sem.at[0]
                    )
                )
    for copy in copies:
        copy.start()
    return copies


def turn(values, cos_ref, sin_ref):
    return values * cos_ref[...] + pltpu.roll(values, HEAD // 2, 1) * sin_ref[...]


def kv_kernel(where, x_ref, docs_ref, cos_ref, sin_ref, *rest):
    pieces, (tile_ref, normed_ref, buffer, sem) = rest[:8], rest[8:]
    copies = load_weights(where, pieces, buffer, sem, 512)
    n_tp, _, cols = x_ref.shape
    rows = normed_ref.shape[0]
    square = jnp.zeros((rows, cols), jnp.float32)
    for j in range(n_tp):
        block = x_ref[j, :rows].astype(jnp.float32)
        square = square + block * block
    scale = lax.rsqrt(jnp.sum(square, axis=1, keepdims=True) / (n_tp * cols) + 1e-05)
    for j in range(n_tp):
        block = x_ref[j, :rows].astype(jnp.float32)
        gain = x_ref[j, pl.ds(rows, 1)].astype(jnp.float32)
        at = FOLDED[j] * cols
        normed_ref[:, at : at + cols] = (block * scale * gain).astype(jnp.bfloat16)
    for copy in copies:
        copy.wait()
    out = jnp.dot(normed_ref[...], buffer[...], preferred_element_type=jnp.float32)
    tile_ref[:rows, :HEAD] = turn(out[:, :HEAD], cos_ref, sin_ref).astype(jnp.bfloat16)
    tile_ref[:rows, HEAD:] = out[:, HEAD:].astype(jnp.bfloat16)
    tile_ref[rows:, :] = docs_ref[...]


def q_kernel(where, normed_ref, cos_ref, sin_ref, *rest):
    pieces, (q_ref, buffer, sem) = rest[:8], rest[8:]
    copies = load_weights(where, pieces, buffer, sem, 0)
    for copy in copies:
        copy.wait()
    out = jnp.dot(normed_ref[...], buffer[...], preferred_element_type=jnp.float32)
    factor = 1.4426950408889634 / HEAD**0.5
    for g in range(q_ref.shape[0]):
        head = turn(out[:, g * HEAD : (g + 1) * HEAD], cos_ref, sin_ref)
        q_ref[g] = (head * factor).astype(jnp.bfloat16)


def attention_kernel(q_ref, docs_ref, mine_ref, other_ref, out_ref, scores):
    group, rows, head = q_ref.shape
    q_docs = docs_ref[...]
    ones = jnp.ones((8, rows, head), jnp.bfloat16)
    for g in range(group):
        at = slice(g * rows, (g + 1) * rows)
        top = None
        for n in range(16):
            ref, s = (mine_ref, n) if n < 8 else (other_ref, n - 8)
            part = lax.dot_general(
                q_ref[g],
                ref[s, :rows, :head],
                (((1,), (1,)), ((), ())),
                preferred_element_type=jnp.float32,
            )
            allowed = ref[s, pl.ds(rows, 1), :].astype(jnp.float32) == q_docs
            if n == 7:
                q_at = lax.broadcasted_iota(jnp.int32, (rows, rows), 0)
                k_at = lax.broadcasted_iota(jnp.int32, (rows, rows), 1)
                allowed = allowed & (k_at <= q_at)
            part = jnp.where(allowed, part, -1e30)
            scores[at, n * rows : (n + 1) * rows] = part
            most = jnp.maximum(part[:, :head], part[:, head:])
            top = most if top is None else jnp.maximum(top, most)
        top = jnp.max(top, axis=1, keepdims=True)
        expw = jnp.exp2(scores[at, :] - top).astype(jnp.bfloat16)
        summed = jnp.zeros((rows, 2 * head), jnp.float32)
        for n, ref in enumerate((mine_ref, other_ref)):
            values = jnp.concatenate([ref[:, :rows, head:], ones], axis=2)
            values = values.reshape(8 * rows, 2 * head)
            summed = summed + jnp.dot(
                expw[:, n * 8 * rows : (n + 1) * 8 * rows], values, preferred_element_type=jnp.float32
            )
        out_ref[:, g * head : (g + 1) * head] = (summed[:, :head] / summed[:, head:]).astype(
            jnp.bfloat16
        )


def out_kernel(zh, a_ref, o_ref, out_ref):
    for n in range(o_ref.shape[0]):
        block = (jnp.where(pl.program_id(0) == 0, n, 3 - n) + 2 * zh[0]) % 4
        out_ref[n] = lax.dot_general(
            a_ref[...], o_ref[block, 0], (((1,), (1,)), ((), ())), preferred_element_type=jnp.float32
        ).astype(jnp.bfloat16)


def local(tokens, norm_gain, doc_ids, q_weight, k_weight, v_weight, o_weight):
    rows, cols = tokens.shape
    n_tp = lax.axis_size("tp")
    q_cols = q_weight.shape[1]
    kv_cols = k_weight.shape[1]
    group = q_cols // HEAD
    zh, y, x, core = (lax.axis_index(a) for a in ("zh", "y", "x", "core"))
    shard = ((zh * 4 + y) * 4 + x) * 2 + core
    where = jnp.stack([zh, y, x, core]).astype(jnp.int32)
    swap = [(0, 1), (1, 0)]

    block = jnp.concatenate([tokens, jnp.broadcast_to(norm_gain[None], (8, cols))], axis=0)
    whole = lax.all_gather(block, "tp", axis=0, tiled=False, axis_index_groups=[FOLDED])

    weight = jnp.concatenate([q_weight, k_weight, v_weight], axis=1)
    away = lax.ppermute(weight, "zh", swap)
    pair = jnp.stack([weight, away])
    near = [pair] + [lax.ppermute(pair, PLANE, plane_route(d, True)) for d in range(1, 4)]
    near = jnp.stack(near)
    pieces = [near] + [lax.ppermute(near, PLANE, plane_route(e, False)) for e in range(1, 4)]

    o_block = o_weight.T
    o_away = lax.ppermute(o_block, "zh", swap)
    o_pair = jnp.stack([o_block, o_away])
    pieces = pieces + [lax.ppermute(piece, "core", swap) for piece in pieces]
    o_rows = lax.all_gather(o_pair, PLANE, axis=1, tiled=True)
    o_rows = o_rows.reshape(n_tp, cols, q_cols)

    inv_freq = 500000.0 ** (-(jnp.arange(HEAD // 2, dtype=jnp.float32) * 2.0) / HEAD)
    positions = (shard * rows + jnp.arange(rows, dtype=jnp.int32)).astype(jnp.float32)
    angles = positions[:, None] * inv_freq[None, :]
    cos_part, sin_part = jnp.cos(angles), jnp.sin(angles)
    cos_part = jnp.concatenate([cos_part, cos_part], axis=1)
    sin_part = jnp.concatenate([-sin_part, sin_part], axis=1)
    docs = doc_ids.astype(jnp.float32) + 1.0
    docs_rows = jnp.broadcast_to(docs[None].astype(jnp.bfloat16), (8, rows))

    vmem, hbm, smem = (pl.BlockSpec(memory_space=s) for s in (pltpu.VMEM, pl.ANY, pltpu.SMEM))
    tile, normed = pl.pallas_call(
        kv_kernel,
        out_shape=(
            jax.ShapeDtypeStruct((rows + 8, 2 * kv_cols), jnp.bfloat16),
            jax.ShapeDtypeStruct((rows, n_tp * cols), jnp.bfloat16),
        ),
        in_specs=[smem, vmem, vmem, vmem, vmem] + [hbm] * 8,
        scratch_shapes=[
            pltpu.VMEM((n_tp * cols, 2 * kv_cols), jnp.bfloat16),
            pltpu.SemaphoreType.DMA((1,)),
        ],
        name="kv_projection",
    )(where, whole, docs_rows, cos_part, sin_part, *pieces)
    q_rot = pl.pallas_call(
        q_kernel,
        out_shape=jax.ShapeDtypeStruct((group, rows, HEAD), jnp.bfloat16),
        in_specs=[smem, vmem, vmem, vmem] + [hbm] * 8,
        scratch_shapes=[
            pltpu.VMEM((n_tp * cols, q_cols), jnp.bfloat16),
            pltpu.SemaphoreType.DMA((1,)),
        ],
        cost_estimate=pl.CostEstimate(
            flops=2 * rows * n_tp * cols * q_cols, bytes_accessed=2 * n_tp * cols * (q_cols + rows), transcendentals=0
        ),
        name="q_projection",
    )(where, normed, cos_part, sin_part, *pieces)

    crossed = lax.ppermute(tile, ("zh", "y"), [(2, 6), (3, 7)])
    carried = (zh == 1) & (y >= 2)
    sent = jnp.where(carried, crossed, tile)
    back_2 = lax.ppermute(sent, ("zh", "y"), [(0, 2), (1, 3), (4, 6), (5, 7), (6, 4), (7, 5)])
    sent = jnp.where(carried & (y == 3), crossed, tile)
    back_1 = lax.ppermute(
        sent, ("zh", "y"), [(0, 1), (1, 2), (2, 3), (4, 5), (5, 6), (6, 7), (7, 4)]
    )
    back_1, back_2, q_rot = lax.optimization_barrier((back_1, back_2, q_rot))
    mine = []
    for step in range(1, 4):
        two = jnp.stack([back_1, jnp.where(x + step < 4, tile, back_2)])
        mine.append(lax.ppermute(two, "x", ring(4, step)))
    sent = mine + [jnp.stack([back_1, jnp.where(core == 0, tile, back_2)])]
    other = lax.ppermute(jnp.concatenate(sent), "core", swap)
    mine = jnp.concatenate(mine + [jnp.stack([back_1, tile])])

    attended = pl.pallas_call(
        attention_kernel,
        out_shape=jax.ShapeDtypeStruct((rows, q_cols), jnp.bfloat16),
        in_specs=[vmem] * 4,
        scratch_shapes=[pltpu.VMEM((group * rows, 16 * rows), jnp.float32)],
        name="attention",
    )(q_rot, docs[:, None], mine, other)

    half = n_tp // 2
    partial_terms = pl.pallas_call(
        out_kernel,
        out_shape=jax.ShapeDtypeStruct((n_tp, rows, cols), jnp.bfloat16),
        grid_spec=pltpu.PrefetchScalarGridSpec(
            num_scalar_prefetch=1,
            grid=(2,),
            in_specs=[
                pl.BlockSpec((rows, q_cols), lambda i, zh: (0, 0)),
                pl.BlockSpec((half, 1, cols, q_cols), lambda i, zh: (0, i, 0, 0)),
            ],
            out_specs=pl.BlockSpec((half, rows, cols), lambda i, zh: (i, 0, 0)),
        ),
        name="out_projection",
    )(where[:1], attended, o_rows.reshape(half, 2, cols, q_cols))
    return lax.psum_scatter(
        partial_terms.reshape(n_tp * rows, cols),
        "tp",
        scatter_dimension=0,
        tiled=True,
        axis_index_groups=[FOLDED],
    )


def solution(mesh):
    fine = Mesh(mesh.devices.reshape(2, 4, 4, 2, 8), ("zh", "y", "x", "core", "tp"))
    ctx = ("zh", "y", "x", "core")
    return jax.shard_map(
        local,
        mesh=fine,
        in_specs=(
            P(ctx, "tp"),
            P("tp"),
            P(ctx),
            P(ctx, "tp"),
            P(ctx, "tp"),
            P(ctx, "tp"),
            P("tp", ctx),
        ),
        out_specs=P(ctx, "tp"),
        check_vma=False,
    )
```
